32 devices in a mesh: seq: 4 (over y, x), img: 2 (over core), dp: 4 (over z).
Axes of the slice: x: 2, y: 2, z: 4, core: 2. Of those that a mesh axis runs over, the one named last changes fastest.
Arguments:
- queries: bfloat16 [512, 8192], P('seq', 'dp'), may hold values from -22 to 22
- out_grad: bfloat16 [512, 8192], P('seq', 'dp'), may hold values from -600 to 600
- token_image: int32 [512], P('seq'), may hold values from -1 to 1, as said below
- unnormed_keys: bfloat16 [2, 6432, 1024], P('img', 'seq', 'dp'), may hold values from -14 to 14
- values: bfloat16 [2, 6432, 1024], P('img', 'seq', 'dp'), may hold values from -6 to 6
- key_gain: float32 [128], replicated, may hold values from 0.1 to 1.9
- tile_count: int32 [2], replicated, may hold values from 1 to 4, as said below
- key_projection_matrix: bfloat16 [8192, 1024], P('dp', 'seq'), may hold values from -0.1875 to 0.1875
- value_projection_matrix: bfloat16 [8192, 1024], P('dp', 'seq'), may hold values from -0.1875 to 0.1875
Outputs:
- feature_grad: bfloat16 [2, 6432, 8192], P('img', 'seq', 'dp')
The draws below stay inside these ranges and needn't reach their ends.
Inputs may be any that keep to these rules, and one draw needn't show every extreme that they name: `token_image`: in each block of 128 tokens (one index of seq) at most 16 tokens name one image, and some image is named by exactly 16; -1 marks a token that attends no image. `tile_count`: some image has 4 tiles.
All inputs are finite; a program needn't handle non-finite values.
Results may differ from the reference program's by a relative error of at most 0.0067.
Values may be sent and summed in bfloat16 or wider, within the bound.
A program may use at most 128 MiB of HBM per device.

```python
import jax
import jax.numpy as jnp
from jax import lax

MODEL_WIDTH = 8192
QUERY_HEAD_COUNT = 64
KEY_VALUE_HEADS = 8
HEAD_WIDTH = 128
TILES = 4
TILE_TOK = 1601
TILE_ROWS = 1608
IMAGE_ROW_COUNT = 6432
TOK_DEV = 128
CAP = 16
IMAGE_COUNT = 2
TEXT_TOKENS = 512
N_SEQ = 4


def image_ids(key):
    random_key_seed = jax.random.fold_in(key, 11)
    blocks = TEXT_TOKENS // TOK_DEV
    group_count = TOK_DEV // CAP
    block_keys = jax.random.split(jax.random.fold_in(random_key_seed, 1), blocks)

    def block_perm(block_key):
        return jax.random.permutation(block_key, IMAGE_COUNT)
    image_perm = jax.vmap(block_perm)(block_keys)
    group_fill = jax.random.randint(jax.random.fold_in(random_key_seed, 2), (blocks, group_count), CAP * 3 // 4, CAP + 1)
    group_fill = jnp.where(jnp.arange(group_count)[None, :] == 0, CAP, group_fill)
    position = jnp.arange(TOK_DEV)
    group_id = position // CAP
    offset = position % CAP
    chosen = image_perm[:, jnp.minimum(group_id, IMAGE_COUNT - 1)]
    is_kept = (group_id[None, :] < IMAGE_COUNT) & (offset[None, :] < group_fill[:, group_id])
    return jnp.where(is_kept, chosen, -1).reshape(TEXT_TOKENS).astype(jnp.int32)


def base_keys(key):
    random_key_seed = jax.random.fold_in(key, 17)
    array_shape = (IMAGE_COUNT, IMAGE_ROW_COUNT, KEY_VALUE_HEADS * HEAD_WIDTH)
    raw_keys = jnp.clip(jax.random.normal(jax.random.fold_in(random_key_seed, 4), array_shape), -6.0, 6.0)
    return raw_keys.astype(jnp.float32)


def draw_token_image(key, part):
    return image_ids(key)


def draw_unnormed_keys(key, part):
    return base_keys(key).astype(jnp.bfloat16)


def draw_tile_count(key, part):
    random_key_seed = jax.random.fold_in(key, 23)
    counts = jax.random.randint(jax.random.fold_in(random_key_seed, 1), (IMAGE_COUNT,), 1, TILES + 1)
    full_image = jax.random.randint(jax.random.fold_in(random_key_seed, 2), (), 0, IMAGE_COUNT)
    image_axis = jnp.arange(IMAGE_COUNT)
    counts = jnp.where(image_axis == full_image, TILES, counts)
    return counts.astype(jnp.int32)


def draw_queries(key, part):
    random_key_seed = jax.random.fold_in(key, 19)
    array_shape = (TEXT_TOKENS, QUERY_HEAD_COUNT * HEAD_WIDTH)
    query_values = jnp.clip(jax.random.normal(jax.random.fold_in(random_key_seed, 5), array_shape), -6.0, 6.0)
    return query_values.astype(jnp.float32).astype(jnp.bfloat16)


def level_of(own_key, dims, shards, low, high):
    def one(dim, parts):
        heights = jax.random.uniform(jax.random.fold_in(jax.random.fold_in(own_key, 6), dim), (parts,), jnp.float32, low / len(shards), high / len(shards))
        return jnp.repeat(jnp.exp(heights), dims[dim] // parts).reshape((-1,) + (1,) * (len(dims) - dim - 1))

    gain = one(*shards[0])
    for cut in shards[1:]:
        gain = gain * one(*cut)
    return gain


def centred(key, dims, spread, bound, shards=(), held_as=jnp.bfloat16):
    gain = level_of(key, dims, shards, -0.22, 0.18) if shards else 1.0
    array = jax.random.normal(key, dims, jnp.float32) * spread * gain
    return jnp.minimum(jnp.maximum(array, -bound), bound).astype(held_as)


def setup_inputs(seed: int = 0) -> dict:
    seeds = jax.random.split(jax.random.key(seed), 10)
    queries = draw_queries(jax.random.fold_in(seeds[9], 71), 0)
    out_grad = centred(seeds[1], (TEXT_TOKENS, QUERY_HEAD_COUNT * HEAD_WIDTH), 100.0, 600.0, ((0, 4), (1, 4)))
    token_image = draw_token_image(jax.random.fold_in(seeds[9], 71), 0)
    unnormed_keys = draw_unnormed_keys(jax.random.fold_in(seeds[9], 71), 0)
    values = centred(seeds[4], (IMAGE_COUNT, IMAGE_ROW_COUNT, KEY_VALUE_HEADS * HEAD_WIDTH), 1.0, 6.0, ((0, 2), (1, 4), (2, 4)))
    key_gain = jnp.clip(1.0 + 0.18 * jax.random.normal(seeds[5], (HEAD_WIDTH,), jnp.float32), 0.1, 1.9)
    tile_count = draw_tile_count(jax.random.fold_in(seeds[9], 71), 0)
    key_projection_matrix = centred(seeds[7], (MODEL_WIDTH, KEY_VALUE_HEADS * HEAD_WIDTH), (KEY_VALUE_HEADS * HEAD_WIDTH) ** -0.5, 0.1875, ((0, 4), (1, 4)))
    value_projection_matrix = centred(seeds[8], (MODEL_WIDTH, KEY_VALUE_HEADS * HEAD_WIDTH), (KEY_VALUE_HEADS * HEAD_WIDTH) ** -0.5, 0.1875, ((0, 4), (1, 4)))
    return dict(queries=queries, out_grad=out_grad, token_image=token_image, unnormed_keys=unnormed_keys, values=values, key_gain=key_gain, tile_count=tile_count, key_projection_matrix=key_projection_matrix, value_projection_matrix=value_projection_matrix)


epsilon = 1e-05
masked = -1e+30

def reference(queries, out_grad, token_image, unnormed_keys, values, key_gain, tile_count, key_projection_matrix, value_projection_matrix):
    group_length = QUERY_HEAD_COUNT // KEY_VALUE_HEADS
    score_scale = HEAD_WIDTH ** (-0.5)
    text_rows = N_SEQ * CAP
    row_ids = jnp.arange(IMAGE_ROW_COUNT, dtype=jnp.int32)
    token_ids = jnp.arange(TEXT_TOKENS, dtype=jnp.int32)
    gain_float = key_gain.astype(jnp.float32)
    contracting = (((1,), (1,)), ((), ()))
    leading = (((0,), (0,)), ((), ()))

    def per_image(image_number):
        attends = token_image == image_number
        text_order = jnp.argsort(jnp.where(attends, token_ids, token_ids + TEXT_TOKENS))[:text_rows].astype(jnp.int32)
        is_valid = attends[text_order][:, None]
        text_query = jnp.where(is_valid, queries[text_order], jnp.zeros((), jnp.bfloat16))
        text_grad = jnp.where(is_valid, out_grad[text_order], jnp.zeros((), jnp.bfloat16))
        unnormed_float = lax.dynamic_index_in_dim(unnormed_keys, image_number, 0, keepdims=False).astype(jnp.float32).reshape(IMAGE_ROW_COUNT, KEY_VALUE_HEADS, HEAD_WIDTH)
        value_row_block = lax.dynamic_index_in_dim(values, image_number, 0, keepdims=False).reshape(IMAGE_ROW_COUNT, KEY_VALUE_HEADS, HEAD_WIDTH)
        inverse = lax.rsqrt(lax.optimization_barrier(jnp.mean(unnormed_float * unnormed_float, axis=-1, keepdims=True)) + epsilon)
        unit_key = unnormed_float * inverse
        normed = (unit_key * gain_float).astype(jnp.bfloat16)
        tile_limit = jnp.sum(jnp.where(jnp.arange(IMAGE_COUNT, dtype=jnp.int32) == image_number, tile_count, 0))
        live_rows = (row_ids // TILE_ROWS < tile_limit) & (row_ids % TILE_ROWS < TILE_TOK)

        def per_head(head_index):
            kv_head = head_index // group_length
            query_head = lax.dynamic_slice_in_dim(text_query, head_index * HEAD_WIDTH, HEAD_WIDTH, 1)
            grad_head = lax.dynamic_slice_in_dim(text_grad, head_index * HEAD_WIDTH, HEAD_WIDTH, 1)
            key_head = lax.dynamic_index_in_dim(normed, kv_head, 1, keepdims=False)
            value_head = lax.dynamic_index_in_dim(value_row_block, kv_head, 1, keepdims=False)
            scores = lax.dot_general(query_head, key_head, contracting, preferred_element_type=jnp.float32) * score_scale
            scores = jnp.where(live_rows[None, :], scores, masked)
            row_top = lax.optimization_barrier(jnp.max(scores, axis=-1, keepdims=True))
            exponent = jnp.exp(scores - row_top)
            probabilities = exponent / lax.optimization_barrier(jnp.sum(exponent, axis=-1, keepdims=True))
            grad_probs = lax.dot_general(grad_head, value_head, contracting, preferred_element_type=jnp.float32)
            inner_sum = lax.optimization_barrier(jnp.sum(probabilities * grad_probs, axis=-1, keepdims=True))
            probs_low = probabilities.astype(jnp.bfloat16)
            score_grad = (probabilities * (grad_probs - inner_sum)).astype(jnp.bfloat16)
            value_part = lax.dot_general(probs_low, grad_head, leading, preferred_element_type=jnp.float32)
            key_part = lax.dot_general(score_grad, query_head, leading, preferred_element_type=jnp.float32) * score_scale
            return (key_part, value_part)
        key_pieces_list, value_pieces_list = lax.map(per_head, jnp.arange(QUERY_HEAD_COUNT, dtype=jnp.int32))
        normalized_gradient = jnp.transpose(key_pieces_list.reshape(KEY_VALUE_HEADS, group_length, IMAGE_ROW_COUNT, HEAD_WIDTH).sum(axis=1), (1, 0, 2))
        value_gradient = jnp.transpose(value_pieces_list.reshape(KEY_VALUE_HEADS, group_length, IMAGE_ROW_COUNT, HEAD_WIDTH).sum(axis=1), (1, 0, 2))
        unit_grad = normalized_gradient * gain_float
        key_gradient = inverse * (unit_grad - unit_key * lax.optimization_barrier(jnp.mean(unit_grad * unit_key, axis=-1, keepdims=True)))
        key_reduced_precision = key_gradient.astype(jnp.bfloat16).reshape(IMAGE_ROW_COUNT, KEY_VALUE_HEADS * HEAD_WIDTH)
        value_reduced_precision = value_gradient.astype(jnp.bfloat16).reshape(IMAGE_ROW_COUNT, KEY_VALUE_HEADS * HEAD_WIDTH)
        feature_out = lax.dot_general(key_reduced_precision, key_projection_matrix, contracting, preferred_element_type=jnp.float32)
        feature_out = feature_out + lax.dot_general(value_reduced_precision, value_projection_matrix, contracting, preferred_element_type=jnp.float32)
        return feature_out.astype(jnp.bfloat16)
    return lax.map(per_image, jnp.arange(IMAGE_COUNT, dtype=jnp.int32))
```

```python
import functools

import jax
import jax.numpy as jnp
from jax import lax
from jax.experimental import pallas as pl
from jax.experimental.pallas import tpu as pltpu
from jax.sharding import PartitionSpec as P

QUERY_HEAD_COUNT = 64
KEY_VALUE_HEADS = 8
HEAD_WIDTH = 128
TILE_TOK = 1601
TILE_ROWS = 1608
CAP = 16


epsilon = 1e-05
masked = -1e30


def body_any(
    queries,
    out_grad,
    token_image,
    unnormed_keys,
    values,
    key_gain,
    tile_count,
    key_projection_matrix,
    value_projection_matrix,
):
    image_number = lax.axis_index("img")
    seq_index = lax.axis_index("seq")
    attends = token_image == image_number
    slot_rank = jnp.cumsum(attends.astype(jnp.int32)) - 1
    picker = (
        attends[None, :] & (slot_rank[None, :] == jnp.arange(CAP, dtype=jnp.int32)[:, None])
    ).astype(jnp.bfloat16)
    packed_query = jnp.dot(picker, queries, preferred_element_type=jnp.float32).astype(jnp.bfloat16)
    packed_grad = jnp.dot(picker, out_grad, preferred_element_type=jnp.float32).astype(jnp.bfloat16)
    text_query, text_grad = (
        lax.all_gather(packed_query, "seq", axis=0, tiled=True),
        lax.all_gather(packed_grad, "seq", axis=0, tiled=True),
    )
    key_rows = unnormed_keys.shape[1]
    key_width = unnormed_keys.shape[2]
    key_heads = key_width // HEAD_WIDTH
    group_length = QUERY_HEAD_COUNT // KEY_VALUE_HEADS
    text_rows = text_query.shape[0]
    score_scale = HEAD_WIDTH ** (-0.5)
    unnormed_float = unnormed_keys[0].astype(jnp.float32).reshape(key_rows, key_heads, HEAD_WIDTH)
    inverse = lax.rsqrt(jnp.mean(unnormed_float * unnormed_float, axis=-1, keepdims=True) + epsilon)
    unit_key = unnormed_float * inverse
    normed = (unit_key * key_gain).astype(jnp.bfloat16)
    value_heads = values[0].reshape(key_rows, key_heads, HEAD_WIDTH)
    query_heads = text_query.reshape(text_rows, key_heads, group_length, HEAD_WIDTH)
    grad_heads = text_grad.reshape(text_rows, key_heads, group_length, HEAD_WIDTH)
    row_global = seq_index * key_rows + jnp.arange(key_rows, dtype=jnp.int32)
    tile_limit = jnp.sum(
        jnp.where(jnp.arange(tile_count.shape[0], dtype=jnp.int32) == image_number, tile_count, 0)
    )
    live_rows = (row_global // TILE_ROWS < tile_limit) & (row_global % TILE_ROWS < TILE_TOK)
    scores = (
        jnp.einsum("rhge,khe->hgrk", query_heads, normed, preferred_element_type=jnp.float32)
        * score_scale
    )
    scores = jnp.where(live_rows, scores, masked)
    grad_probs = jnp.einsum(
        "rhge,khe->hgrk", grad_heads, value_heads, preferred_element_type=jnp.float32
    )
    row_top = lax.pmax(jnp.max(scores, axis=-1), "seq")
    exponent = jnp.exp(scores - row_top[..., None])
    row_total = lax.psum(jnp.sum(exponent, axis=-1), "seq")
    probabilities = exponent / row_total[..., None]
    inner_sum = lax.psum(jnp.sum(probabilities * grad_probs, axis=-1), "seq")
    probs_low = probabilities.astype(jnp.bfloat16)
    score_grad = (probabilities * (grad_probs - inner_sum[..., None])).astype(jnp.bfloat16)
    value_gradient = jnp.einsum(
        "hgrk,rhge->khe", probs_low, grad_heads, preferred_element_type=jnp.float32
    )
    normalized_gradient = (
        jnp.einsum("hgrk,rhge->khe", score_grad, query_heads, preferred_element_type=jnp.float32)
        * score_scale
    )
    unit_grad = normalized_gradient * key_gain
    key_gradient = inverse * (
        unit_grad - unit_key * jnp.mean(unit_grad * unit_key, axis=-1, keepdims=True)
    )
    key_reduced_precision = key_gradient.astype(jnp.bfloat16).reshape(key_rows, key_width)
    value_reduced_precision = value_gradient.astype(jnp.bfloat16).reshape(key_rows, key_width)
    key_all, value_all = (
        lax.all_gather(key_reduced_precision, "dp", axis=1, tiled=True),
        lax.all_gather(value_reduced_precision, "dp", axis=1, tiled=True),
    )
    contracting = (((1,), (1,)), ((), ()))
    partial_value = lax.dot_general(
        key_all,
        lax.all_gather(key_projection_matrix, "seq", axis=1, tiled=True),
        contracting,
        preferred_element_type=jnp.float32,
    )
    feature_sum = partial_value + lax.dot_general(
        value_all,
        lax.all_gather(value_projection_matrix, "seq", axis=1, tiled=True),
        contracting,
        preferred_element_type=jnp.float32,
    )
    return feature_sum.astype(jnp.bfloat16)[None]


MESH = pl.DeviceIdType.MESH
NT = (((1,), (1,)), ((), ()))
NN = (((1,), (0,)), ((), ()))
CHUNK = 272
FEATURE_TILE = 256


def dot(a, b, dims):
    return lax.dot_general(a, b, dims, preferred_element_type=jnp.float32)


def kernel(
    sizes,
    image_ref,
    limit_ref,
    query_ref,
    grad_ref,
    key_ref,
    value_ref,
    gain_ref,
    key_weight_ref,
    value_weight_ref,
    out_ref,
    text,
    score,
    grad_prob,
    stats,
    rows_all,
    weights,
    text_send,
    text_recv,
    stat_send,
    stat_recv,
    weight_local,
    weight_send,
    weight_recv,
    relay_send,
    relay_recv,
    row_send,
    row_recv,
):
    n_seq, n_dp, heads, group = sizes
    seq = lax.axis_index("seq")
    img = lax.axis_index("img")
    dp = lax.axis_index("dp")
    rows, width = key_ref.shape
    features = key_weight_ref.shape[0]
    half = features // 2
    stack = group * CAP
    query_rows = n_seq * stack
    full = rows // CHUNK
    rest = rows - full * CHUNK
    padded = rows_all.shape[1]
    chunks = [(c * CHUNK, CHUNK) for c in range(full)] + [(full * CHUNK, padded - full * CHUNK)]
    scale = HEAD_WIDTH ** (-0.5)
    seq_peers = [lax.rem(seq + j, n_seq) for j in range(1, n_seq)]

    own_weights = [
        pltpu.make_async_copy(
            ref, weights.at[seq, :, pl.ds(k * width, width)], weight_local.at[k]
        )
        for k, ref in enumerate((key_weight_ref, value_weight_ref))
    ]
    for copy in own_weights:
        copy.start()

    barrier = pltpu.get_barrier_semaphore()
    for peer in seq_peers:
        pl.semaphore_signal(barrier, inc=1, device_id={"seq": peer}, device_id_type=MESH)
    pl.semaphore_signal(barrier, inc=1, device_id={"img": 1 - img}, device_id_type=MESH)
    for j in range(1, n_dp):
        pl.semaphore_signal(
            barrier, inc=1, device_id={"dp": lax.rem(dp + j, n_dp)}, device_id_type=MESH
        )

    tokens = image_ref.shape[1]
    attends = image_ref[...] == img
    upper = (
        lax.broadcasted_iota(jnp.int32, (tokens, tokens), 0)
        <= lax.broadcasted_iota(jnp.int32, (tokens, tokens), 1)
    ).astype(jnp.bfloat16)
    counts = dot(
        jnp.broadcast_to(attends.astype(jnp.float32), (CAP, tokens)).astype(jnp.bfloat16), upper, NN
    )
    slot = lax.broadcasted_iota(jnp.int32, (CAP, tokens), 0).astype(jnp.float32) + 1.0
    picker = jnp.where(attends & (counts == slot), 1.0, 0.0).astype(jnp.bfloat16)
    for k, ref in enumerate((query_ref, grad_ref)):
        packed = dot(picker, ref[...], NN).astype(jnp.bfloat16)
        for h in range(heads):
            for g in range(group):
                column = (h * group + g) * HEAD_WIDTH
                text[seq, k, h, g * CAP : (g + 1) * CAP, :] = packed[:, column : column + HEAD_WIDTH]

    pl.semaphore_wait(barrier, n_seq - 1 + 1 + n_dp - 1)

    def text_copy(owner, peer, j):
        return pltpu.make_async_remote_copy(
            src_ref=text.at[owner],
            dst_ref=text.at[owner],
            send_sem=text_send.at[j],
            recv_sem=text_recv.at[owner],
            device_id={"seq": peer},
            device_id_type=MESH,
        )

    for j, peer in enumerate(seq_peers):
        text_copy(seq, peer, j).start()

    gain = gain_ref[...]
    live_limit = limit_ref[0]

    def unit_of(row0, size, h):
        k = key_ref[pl.ds(row0, size), h * HEAD_WIDTH : (h + 1) * HEAD_WIDTH].astype(jnp.float32)
        inverse = lax.rsqrt(jnp.mean(k * k, axis=-1, keepdims=True) + epsilon)
        return k * inverse, inverse

    for j, peer in enumerate(seq_peers):
        text_copy(peer, peer, j).wait_recv()

    def heads_of(k, h):
        return text[:, k, h].reshape(query_rows, HEAD_WIDTH)

    def first_pass(row0, size, tops):
        new_tops = []
        local = row0 + lax.broadcasted_iota(jnp.int32, (size, 1), 0)
        row = seq * rows + local
        live = (row // TILE_ROWS < live_limit) & (row % TILE_ROWS < TILE_TOK)
        for h in range(heads):
            unit, _ = unit_of(row0, size, h)
            normed = (unit * gain).astype(jnp.bfloat16)
            s = jnp.where(live, dot(normed, heads_of(0, h), NT) * scale, masked)
            score[h, pl.ds(row0, size), :] = s
            new_tops.append(jnp.maximum(tops[h], jnp.max(s, axis=0, keepdims=True)))
        return tuple(new_tops)

    tops = tuple(jnp.full((1, query_rows), masked, jnp.float32) for _ in range(heads))
    tops = lax.fori_loop(
        0, full, lambda i, c: first_pass(pl.multiple_of(i * CHUNK, 16), CHUNK, c), tops
    )
    tops = first_pass(full * CHUNK, rest, tops)

    def second_pass(row0, size, sums):
        new_sums = []
        for h in range(heads):
            e = jnp.exp(score[h, pl.ds(row0, size), :] - tops[h])
            v = value_ref[pl.ds(row0, size), h * HEAD_WIDTH : (h + 1) * HEAD_WIDTH]
            p = dot(v, heads_of(1, h), NT)
            score[h, pl.ds(row0, size), :] = e
            grad_prob[h, pl.ds(row0, size), :] = p
            new_sums.append(sums[2 * h] + jnp.sum(e, axis=0, keepdims=True))
            new_sums.append(sums[2 * h + 1] + jnp.sum(e * p, axis=0, keepdims=True))
        return tuple(new_sums)

    sums = tuple(jnp.zeros((1, query_rows), jnp.float32) for _ in range(2 * heads))
    sums = lax.fori_loop(
        0, full, lambda i, c: second_pass(pl.multiple_of(i * CHUNK, 16), CHUNK, c), sums
    )
    sums = second_pass(full * CHUNK, rest, sums)
    for h in range(heads):
        columns = slice(h * query_rows, (h + 1) * query_rows)
        stats[seq, 0:1, columns] = tops[h]
        stats[seq, 1:2, columns] = sums[2 * h]
        stats[seq, 2:3, columns] = sums[2 * h + 1]
        stats[seq, 3:8, columns] = jnp.zeros((5, query_rows), jnp.float32)

    def stat_copy(owner, peer, j):
        return pltpu.make_async_remote_copy(
            src_ref=stats.at[owner],
            dst_ref=stats.at[owner],
            send_sem=stat_send.at[j],
            recv_sem=stat_recv.at[owner],
            device_id={"seq": peer},
            device_id_type=MESH,
        )

    for j, peer in enumerate(seq_peers):
        stat_copy(seq, peer, j).start()
    for copy in own_weights:
        copy.wait()
    for j, peer in enumerate(seq_peers):
        stat_copy(peer, peer, j).wait_recv()

    def weight_copy(owner, peer, j):
        part = weights.at[owner, pl.ds(pl.multiple_of(img * half, half), half)]
        return pltpu.make_async_remote_copy(
            src_ref=part,
            dst_ref=part,
            send_sem=weight_send.at[j],
            recv_sem=weight_recv.at[owner],
            device_id={"seq": peer},
            device_id_type=MESH,
        )

    def relay_copy(owner, j, which):
        part = weights.at[owner, pl.ds(pl.multiple_of(which * half, half), half)]
        return pltpu.make_async_remote_copy(
            src_ref=part,
            dst_ref=part,
            send_sem=relay_send.at[j],
            recv_sem=relay_recv.at[owner],
            device_id={"img": 1 - img},
            device_id_type=MESH,
        )

    for j, peer in enumerate(seq_peers):
        weight_copy(seq, peer, j).start()

    all_tops = [stats[i, 0:1, :] for i in range(n_seq)]
    top = functools.reduce(jnp.maximum, all_tops)
    factors = [jnp.exp(t - top) for t in all_tops]
    total = sum(f * stats[i, 1:2, :] for i, f in enumerate(factors))
    inner_all = sum(f * stats[i, 2:3, :] for i, f in enumerate(factors)) / total
    own_factor_all = jnp.exp(stats[seq, 0:1, :] - top) / total

    def row_copy(owner, row0, size, c, side, distance):
        part = rows_all.at[owner, pl.ds(row0, size)]
        return pltpu.make_async_remote_copy(
            src_ref=part,
            dst_ref=part,
            send_sem=row_send.at[side, distance, c],
            recv_sem=row_recv.at[owner, c],
            device_id={"dp": dp + 1 if side == 0 else dp - 1},
            device_id_type=MESH,
        )

    def forward(row0, size, c, distance, act):
        for side in range(2):
            owner = dp - distance if side == 0 else dp + distance
            if side == 0:
                sends = (owner >= 0) & (dp < n_dp - 1)
            else:
                sends = (owner < n_dp) & (dp > 0)

            @pl.when(sends)
            def _():
                act(row_copy(owner, row0, size, c, side, distance))

    def arrive(row0, size, c, distance):
        for side in range(2):
            owner = dp - distance if side == 0 else dp + distance

            @pl.when((owner >= 0) & (owner < n_dp))
            def _():
                row_copy(owner, row0, size, c, side, 0).wait_recv()

    def third_pass(row0, size):
        for h in range(heads):
            columns = slice(h * query_rows, (h + 1) * query_rows)
            p = score[h, pl.ds(row0, size), :] * own_factor_all[:, columns]
            g = (p * (grad_prob[h, pl.ds(row0, size), :] - inner_all[:, columns])).astype(jnp.bfloat16)
            value_gradient = dot(p.astype(jnp.bfloat16), heads_of(1, h), NN)
            unit_grad = dot(g, heads_of(0, h), NN) * scale * gain
            unit, inverse = unit_of(row0, size, h)
            key_gradient = inverse * (
                unit_grad - unit * jnp.mean(unit_grad * unit, axis=-1, keepdims=True)
            )
            lane = h * HEAD_WIDTH
            rows_all[dp, pl.ds(row0, size), lane : lane + HEAD_WIDTH] = key_gradient.astype(
                jnp.bfloat16
            )
            lane = lane + width
            rows_all[dp, pl.ds(row0, size), lane : lane + HEAD_WIDTH] = value_gradient.astype(
                jnp.bfloat16
            )

    def start(copy):
        copy.start()

    def own_chunk(i, _):
        row0 = pl.multiple_of(i * CHUNK, 16)
        third_pass(row0, CHUNK)
        forward(row0, CHUNK, i, 0, start)
        return 0

    lax.fori_loop(0, full, own_chunk, 0)
    third_pass(full * CHUNK, rest)
    forward(chunks[-1][0], chunks[-1][1], full, 0, start)

    for c, (row0, size) in enumerate(chunks):
        arrive(row0, size, c, 1)
        forward(row0, size, c, 1, start)
    for j, peer in enumerate(seq_peers):
        weight_copy(peer, peer, j).wait_recv()
        relay_copy(peer, j, img).start()
    for c, (row0, size) in enumerate(chunks):
        arrive(row0, size, c, 2)
        forward(row0, size, c, 2, start)
    for j, peer in enumerate(seq_peers):
        relay_copy(peer, j, 1 - img).wait_recv()

    def multiply(row0, size):
        def tile(i, _):
            column = pl.multiple_of(i * FEATURE_TILE, FEATURE_TILE)
            total = functools.reduce(
                jnp.add,
                [
                    dot(
                        rows_all[b, pl.ds(row0, size), :],
                        weights[b, pl.ds(column, FEATURE_TILE), :],
                        NT,
                    )
                    for b in range(n_dp)
                ],
            )
            out_ref[pl.ds(row0, size), pl.ds(column, FEATURE_TILE)] = total.astype(out_ref.dtype)
            return 0

        lax.fori_loop(0, features // FEATURE_TILE, tile, 0)

    def finish_chunk(i, _):
        row0 = pl.multiple_of(i * CHUNK, 16)
        arrive(row0, CHUNK, i, 3)
        multiply(row0, CHUNK)
        return 0

    lax.fori_loop(0, full, finish_chunk, 0)
    arrive(chunks[-1][0], chunks[-1][1], full, 3)
    multiply(full * CHUNK, rest)

    def sent(copy):
        copy.wait_send()

    for c, (row0, size) in enumerate(chunks):
        for distance in range(n_dp - 1):
            forward(row0, size, c, distance, sent)
    for j, peer in enumerate(seq_peers):
        text_copy(seq, peer, j).wait_send()
        stat_copy(seq, peer, j).wait_send()
        weight_copy(seq, peer, j).wait_send()
        relay_copy(peer, j, img).wait_send()


def body_kernel(
    sizes,
    queries,
    out_grad,
    token_image,
    unnormed_keys,
    values,
    key_gain,
    tile_count,
    key_projection_matrix,
    value_projection_matrix,
):
    n_seq, n_dp, heads, group = sizes
    rows, width = unnormed_keys.shape[1:]
    features = key_projection_matrix.shape[0]
    query_rows = n_seq * group * CAP
    chunk_count = rows // CHUNK + 1
    padded = -(-rows // 16) * 16
    tile_limit = lax.dynamic_slice_in_dim(tile_count, lax.axis_index("img"), 1)
    vmem = pl.BlockSpec(memory_space=pltpu.VMEM)
    anywhere = pl.BlockSpec(memory_space=pl.ANY)
    dma = pltpu.SemaphoreType.DMA
    result = pl.pallas_call(
        functools.partial(kernel, sizes),
        out_shape=jax.ShapeDtypeStruct((rows, features), jnp.bfloat16),
        in_specs=[
            vmem,
            pl.BlockSpec(memory_space=pltpu.SMEM),
            vmem,
            vmem,
            vmem,
            vmem,
            vmem,
            anywhere,
            anywhere,
        ],
        out_specs=vmem,
        scratch_shapes=[
            pltpu.VMEM((n_seq, 2, heads, group * CAP, HEAD_WIDTH), jnp.bfloat16),
            pltpu.VMEM((heads, rows, query_rows), jnp.float32),
            pltpu.VMEM((heads, rows, query_rows), jnp.float32),
            pltpu.VMEM((n_seq, 8, heads * query_rows), jnp.float32),
            pltpu.VMEM((n_dp, padded, 2 * width), jnp.bfloat16),
            pltpu.VMEM((n_seq, features, 2 * width), jnp.bfloat16),
            dma((n_seq - 1,)),
            dma((n_seq,)),
            dma((n_seq - 1,)),
            dma((n_seq,)),
            dma((2,)),
            dma((n_seq - 1,)),
            dma((n_seq,)),
            dma((n_seq - 1,)),
            dma((n_seq,)),
            dma((2, n_dp - 1, chunk_count)),
            dma((n_dp, chunk_count)),
        ],
        compiler_params=pltpu.CompilerParams(
            collective_id=0, has_side_effects=True, vmem_limit_bytes=60 * 1024 * 1024
        ),
    )(
        token_image[None],
        tile_limit,
        queries,
        out_grad,
        unnormed_keys[0],
        values[0],
        key_gain[None],
        key_projection_matrix,
        value_projection_matrix,
    )
    return result[None]


def body(*args):
    n_seq, n_img, n_dp = (lax.axis_size(name) for name in ("seq", "img", "dp"))
    rows, width = args[3].shape[1:]
    heads = width // HEAD_WIDTH
    group = args[0].shape[1] // width
    fits = n_img == 2 and n_seq == n_dp == 4 and args[7].shape[1] == width and rows % 8 == 0
    if fits and rows % CHUNK and rows % CHUNK % 16 == 8:
        return body_kernel((n_seq, n_dp, heads, group), *args)
    return body_any(*args)


def solution(mesh):
    in_specs = (
        P("seq", "dp"),
        P("seq", "dp"),
        P("seq"),
        P("img", "seq", "dp"),
        P("img", "seq", "dp"),
        P(),
        P(),
        P("dp", "seq"),
        P("dp", "seq"),
    )
    out_specs = P("img", "seq", "dp")
    return jax.shard_map(body, mesh=mesh, in_specs=in_specs, out_specs=out_specs, check_vma=False)
```

```python
import functools

import jax
import jax.numpy as jnp
from jax import lax
from jax.experimental import pallas as pl
from jax.experimental.pallas import tpu as pltpu
from jax.sharding import PartitionSpec as P

QUERY_HEAD_COUNT = 64
KEY_VALUE_HEADS = 8
HEAD_WIDTH = 128
TILE_TOK = 1601
TILE_ROWS = 1608
CAP = 16


epsilon = 1e-05
masked = -1e30


def body_any(
    queries,
    out_grad,
    token_image,
    unnormed_keys,
    values,
    key_gain,
    tile_count,
    key_projection_matrix,
    value_projection_matrix,
):
    image_number = lax.axis_index("img")
    seq_index = lax.axis_index("seq")
    attends = token_image == image_number
    slot_rank = jnp.cumsum(attends.astype(jnp.int32)) - 1
    picker = (
        attends[None, :] & (slot_rank[None, :] == jnp.arange(CAP, dtype=jnp.int32)[:, None])
    ).astype(jnp.bfloat16)
    packed_query = jnp.dot(picker, queries, preferred_element_type=jnp.float32).astype(jnp.bfloat16)
    packed_grad = jnp.dot(picker, out_grad, preferred_element_type=jnp.float32).astype(jnp.bfloat16)
    text_query, text_grad = (
        lax.all_gather(packed_query, "seq", axis=0, tiled=True),
        lax.all_gather(packed_grad, "seq", axis=0, tiled=True),
    )
    key_rows = unnormed_keys.shape[1]
    key_width = unnormed_keys.shape[2]
    key_heads = key_width // HEAD_WIDTH
    group_length = QUERY_HEAD_COUNT // KEY_VALUE_HEADS
    text_rows = text_query.shape[0]
    score_scale = HEAD_WIDTH ** (-0.5)
    unnormed_float = unnormed_keys[0].astype(jnp.float32).reshape(key_rows, key_heads, HEAD_WIDTH)
    inverse = lax.rsqrt(jnp.mean(unnormed_float * unnormed_float, axis=-1, keepdims=True) + epsilon)
    unit_key = unnormed_float * inverse
    normed = (unit_key * key_gain).astype(jnp.bfloat16)
    value_heads = values[0].reshape(key_rows, key_heads, HEAD_WIDTH)
    query_heads = text_query.reshape(text_rows, key_heads, group_length, HEAD_WIDTH)
    grad_heads = text_grad.reshape(text_rows, key_heads, group_length, HEAD_WIDTH)
    row_global = seq_index * key_rows + jnp.arange(key_rows, dtype=jnp.int32)
    tile_limit = jnp.sum(
        jnp.where(jnp.arange(tile_count.shape[0], dtype=jnp.int32) == image_number, tile_count, 0)
    )
    live_rows = (row_global // TILE_ROWS < tile_limit) & (row_global % TILE_ROWS < TILE_TOK)
    scores = (
        jnp.einsum("rhge,khe->hgrk", query_heads, normed, preferred_element_type=jnp.float32)
        * score_scale
    )
    scores = jnp.where(live_rows, scores, masked)
    grad_probs = jnp.einsum(
        "rhge,khe->hgrk", grad_heads, value_heads, preferred_element_type=jnp.float32
    )
    row_top = lax.pmax(jnp.max(scores, axis=-1), "seq")
    exponent = jnp.exp(scores - row_top[..., None])
    row_total = lax.psum(jnp.sum(exponent, axis=-1), "seq")
    probabilities = exponent / row_total[..., None]
    inner_sum = lax.psum(jnp.sum(probabilities * grad_probs, axis=-1), "seq")
    probs_low = probabilities.astype(jnp.bfloat16)
    score_grad = (probabilities * (grad_probs - inner_sum[..., None])).astype(jnp.bfloat16)
    value_gradient = jnp.einsum(
        "hgrk,rhge->khe", probs_low, grad_heads, preferred_element_type=jnp.float32
    )
    normalized_gradient = (
        jnp.einsum("hgrk,rhge->khe", score_grad, query_heads, preferred_element_type=jnp.float32)
        * score_scale
    )
    unit_grad = normalized_gradient * key_gain
    key_gradient = inverse * (
        unit_grad - unit_key * jnp.mean(unit_grad * unit_key, axis=-1, keepdims=True)
    )
    key_reduced_precision = key_gradient.astype(jnp.bfloat16).reshape(key_rows, key_width)
    value_reduced_precision = value_gradient.astype(jnp.bfloat16).reshape(key_rows, key_width)
    key_all, value_all = (
        lax.all_gather(key_reduced_precision, "dp", axis=1, tiled=True),
        lax.all_gather(value_reduced_precision, "dp", axis=1, tiled=True),
    )
    contracting = (((1,), (1,)), ((), ()))
    partial_value = lax.dot_general(
        key_all,
        lax.all_gather(key_projection_matrix, "seq", axis=1, tiled=True),
        contracting,
        preferred_element_type=jnp.float32,
    )
    feature_sum = partial_value + lax.dot_general(
        value_all,
        lax.all_gather(value_projection_matrix, "seq", axis=1, tiled=True),
        contracting,
        preferred_element_type=jnp.float32,
    )
    return feature_sum.astype(jnp.bfloat16)[None]


MESH = pl.DeviceIdType.MESH
NT = (((1,), (1,)), ((), ()))
NN = (((1,), (0,)), ((), ()))
CHUNK = 272
FEATURE_TILE = 256


def dot(a, b, dims):
    return lax.dot_general(a, b, dims, preferred_element_type=jnp.float32)


def kernel(
    sizes,
    image_ref,
    limit_ref,
    query_ref,
    grad_ref,
    key_ref,
    value_ref,
    gain_ref,
    key_weight_ref,
    value_weight_ref,
    out_ref,
    text,
    score,
    grad_prob,
    stats,
    rows_all,
    weights,
    text_send,
    text_recv,
    stat_send,
    stat_recv,
    weight_local,
    weight_send,
    weight_recv,
    relay_send,
    relay_recv,
    row_send,
    row_recv,
):
    n_seq, n_dp, heads, group = sizes
    seq = lax.axis_index("seq")
    img = lax.axis_index("img")
    dp = lax.axis_index("dp")
    rows, width = key_ref.shape
    features = key_weight_ref.shape[0]
    half = features // 2
    stack = group * CAP
    query_rows = n_seq * stack
    full = rows // CHUNK
    rest = rows - full * CHUNK
    padded = rows_all.shape[1]
    chunks = [(c * CHUNK, CHUNK) for c in range(full)] + [(full * CHUNK, padded - full * CHUNK)]
    scale = HEAD_WIDTH ** (-0.5)
    seq_peers = [lax.rem(seq + j, n_seq) for j in range(1, n_seq)]

    own_weights = [
        pltpu.make_async_copy(
            ref, weights.at[seq, :, pl.ds(k * width, width)], weight_local.at[k]
        )
        for k, ref in enumerate((key_weight_ref, value_weight_ref))
    ]
    for copy in own_weights:
        copy.start()

    barrier = pltpu.get_barrier_semaphore()
    for peer in seq_peers:
        pl.semaphore_signal(barrier, inc=1, device_id={"seq": peer}, device_id_type=MESH)
    pl.semaphore_signal(barrier, inc=1, device_id={"img": 1 - img}, device_id_type=MESH)
    for j in range(1, n_dp):
        pl.semaphore_signal(
            barrier, inc=1, device_id={"dp": lax.rem(dp + j, n_dp)}, device_id_type=MESH
        )

    tokens = image_ref.shape[1]
    attends = image_ref[...] == img
    upper = (
        lax.broadcasted_iota(jnp.int32, (tokens, tokens), 0)
        <= lax.broadcasted_iota(jnp.int32, (tokens, tokens), 1)
    ).astype(jnp.bfloat16)
    counts = dot(
        jnp.broadcast_to(attends.astype(jnp.float32), (CAP, tokens)).astype(jnp.bfloat16), upper, NN
    )
    slot = lax.broadcasted_iota(jnp.int32, (CAP, tokens), 0).astype(jnp.float32) + 1.0
    picker = jnp.where(attends & (counts == slot), 1.0, 0.0).astype(jnp.bfloat16)
    for k, ref in enumerate((query_ref, grad_ref)):
        packed = dot(picker, ref[...], NN).astype(jnp.bfloat16)
        for h in range(heads):
            for g in range(group):
                column = (h * group + g) * HEAD_WIDTH
                text[seq, k, h, g * CAP : (g + 1) * CAP, :] = packed[:, column : column + HEAD_WIDTH]

    pl.semaphore_wait(barrier, n_seq - 1 + 1 + n_dp - 1)

    def text_copy(owner, peer, j):
        return pltpu.make_async_remote_copy(
            src_ref=text.at[owner],
            dst_ref=text.at[owner],
            send_sem=text_send.at[j],
            recv_sem=text_recv.at[owner],
            device_id={"seq": peer},
            device_id_type=MESH,
        )

    for j, peer in enumerate(seq_peers):
        text_copy(seq, peer, j).start()

    gain = gain_ref[...]
    live_limit = limit_ref[img]

    def unit_of(row0, size, h):
        k = key_ref[pl.ds(row0, size), h * HEAD_WIDTH : (h + 1) * HEAD_WIDTH].astype(jnp.float32)
        inverse = lax.rsqrt(jnp.mean(k * k, axis=-1, keepdims=True) + epsilon)
        return k * inverse, inverse

    for j, peer in enumerate(seq_peers):
        text_copy(peer, peer, j).wait_recv()

    def heads_of(k, h):
        return text[:, k, h].reshape(query_rows, HEAD_WIDTH)

    def first_pass(row0, size, tops):
        new_tops = []
        local = row0 + lax.broadcasted_iota(jnp.int32, (size, 1), 0)
        row = seq * rows + local
        live = (row // TILE_ROWS < live_limit) & (row % TILE_ROWS < TILE_TOK)
        for h in range(heads):
            unit, _ = unit_of(row0, size, h)
            normed = (unit * gain).astype(jnp.bfloat16)
            s = jnp.where(live, dot(normed, heads_of(0, h), NT) * scale, masked)
            score[h, pl.ds(row0, size), :] = s
            new_tops.append(jnp.maximum(tops[h], jnp.max(s, axis=0, keepdims=True)))
        return tuple(new_tops)

    tops = tuple(jnp.full((1, query_rows), masked, jnp.float32) for _ in range(heads))
    tops = lax.fori_loop(
        0, full, lambda i, c: first_pass(pl.multiple_of(i * CHUNK, 16), CHUNK, c), tops
    )
    tops = first_pass(full * CHUNK, rest, tops)

    def second_pass(row0, size, sums):
        new_sums = []
        for h in range(heads):
            e = jnp.exp(score[h, pl.ds(row0, size), :] - tops[h])
            v = value_ref[pl.ds(row0, size), h * HEAD_WIDTH : (h + 1) * HEAD_WIDTH]
            p = dot(v, heads_of(1, h), NT)
            score[h, pl.ds(row0, size), :] = e
            grad_prob[h, pl.ds(row0, size), :] = p
            new_sums.append(sums[2 * h] + jnp.sum(e, axis=0, keepdims=True))
            new_sums.append(sums[2 * h + 1] + jnp.sum(e * p, axis=0, keepdims=True))
        return tuple(new_sums)

    sums = tuple(jnp.zeros((1, query_rows), jnp.float32) for _ in range(2 * heads))
    sums = lax.fori_loop(
        0, full, lambda i, c: second_pass(pl.multiple_of(i * CHUNK, 16), CHUNK, c), sums
    )
    sums = second_pass(full * CHUNK, rest, sums)
    for h in range(heads):
        columns = slice(h * query_rows, (h + 1) * query_rows)
        stats[seq, 0:1, columns] = tops[h]
        stats[seq, 1:2, columns] = sums[2 * h]
        stats[seq, 2:3, columns] = sums[2 * h + 1]
        stats[seq, 3:8, columns] = jnp.zeros((5, query_rows), jnp.float32)

    def stat_copy(owner, peer, j):
        return pltpu.make_async_remote_copy(
            src_ref=stats.at[owner],
            dst_ref=stats.at[owner],
            send_sem=stat_send.at[j],
            recv_sem=stat_recv.at[owner],
            device_id={"seq": peer},
            device_id_type=MESH,
        )

    for j, peer in enumerate(seq_peers):
        stat_copy(seq, peer, j).start()
    for copy in own_weights:
        copy.wait()
    for j, peer in enumerate(seq_peers):
        stat_copy(peer, peer, j).wait_recv()

    def weight_copy(owner, peer, j):
        part = weights.at[owner, pl.ds(pl.multiple_of(img * half, half), half)]
        return pltpu.make_async_remote_copy(
            src_ref=part,
            dst_ref=part,
            send_sem=weight_send.at[j],
            recv_sem=weight_recv.at[owner],
            device_id={"seq": peer},
            device_id_type=MESH,
        )

    def relay_copy(owner, j, which):
        part = weights.at[owner, pl.ds(pl.multiple_of(which * half, half), half)]
        return pltpu.make_async_remote_copy(
            src_ref=part,
            dst_ref=part,
            send_sem=relay_send.at[j],
            recv_sem=relay_recv.at[owner],
            device_id={"img": 1 - img},
            device_id_type=MESH,
        )

    for j, peer in enumerate(seq_peers):
        weight_copy(seq, peer, j).start()

    all_tops = [stats[i, 0:1, :] for i in range(n_seq)]
    top = functools.reduce(jnp.maximum, all_tops)
    factors = [jnp.exp(t - top) for t in all_tops]
    total = sum(f * stats[i, 1:2, :] for i, f in enumerate(factors))
    inner_all = sum(f * stats[i, 2:3, :] for i, f in enumerate(factors)) / total
    own_factor_all = jnp.exp(stats[seq, 0:1, :] - top) / total

    def row_copy(owner, row0, size, c, side, distance):
        part = rows_all.at[owner, pl.ds(row0, size)]
        return pltpu.make_async_remote_copy(
            src_ref=part,
            dst_ref=part,
            send_sem=row_send.at[side, distance, c],
            recv_sem=row_recv.at[owner, c],
            device_id={"dp": dp + 1 if side == 0 else dp - 1},
            device_id_type=MESH,
        )

    def forward(row0, size, c, distance, act):
        for side in range(2):
            owner = dp - distance if side == 0 else dp + distance
            if side == 0:
                sends = (owner >= 0) & (dp < n_dp - 1)
            else:
                sends = (owner < n_dp) & (dp > 0)

            @pl.when(sends)
            def _():
                act(row_copy(owner, row0, size, c, side, distance))

    def arrive(row0, size, c, distance):
        for side in range(2):
            owner = dp - distance if side == 0 else dp + distance

            @pl.when((owner >= 0) & (owner < n_dp))
            def _():
                row_copy(owner, row0, size, c, side, 0).wait_recv()

    def third_pass(row0, size):
        for h in range(heads):
            columns = slice(h * query_rows, (h + 1) * query_rows)
            p = score[h, pl.ds(row0, size), :] * own_factor_all[:, columns]
            g = (p * (grad_prob[h, pl.ds(row0, size), :] - inner_all[:, columns])).astype(jnp.bfloat16)
            value_gradient = dot(p.astype(jnp.bfloat16), heads_of(1, h), NN)
            unit_grad = dot(g, heads_of(0, h), NN) * scale * gain
            unit, inverse = unit_of(row0, size, h)
            key_gradient = inverse * (
                unit_grad - unit * jnp.mean(unit_grad * unit, axis=-1, keepdims=True)
            )
            lane = h * HEAD_WIDTH
            rows_all[dp, pl.ds(row0, size), lane : lane + HEAD_WIDTH] = key_gradient.astype(
                jnp.bfloat16
            )
            lane = lane + width
            rows_all[dp, pl.ds(row0, size), lane : lane + HEAD_WIDTH] = value_gradient.astype(
                jnp.bfloat16
            )

    def start(copy):
        copy.start()

    def own_chunk(i, _):
        row0 = pl.multiple_of(i * CHUNK, 16)
        third_pass(row0, CHUNK)
        forward(row0, CHUNK, i, 0, start)
        return 0

    lax.fori_loop(0, full, own_chunk, 0)
    third_pass(full * CHUNK, rest)
    forward(chunks[-1][0], chunks[-1][1], full, 0, start)

    for c, (row0, size) in enumerate(chunks):
        arrive(row0, size, c, 1)
        forward(row0, size, c, 1, start)
    for j, peer in enumerate(seq_peers):
        weight_copy(peer, peer, j).wait_recv()
        relay_copy(peer, j, img).start()
    for c, (row0, size) in enumerate(chunks):
        arrive(row0, size, c, 2)
        forward(row0, size, c, 2, start)
    for j, peer in enumerate(seq_peers):
        relay_copy(peer, j, 1 - img).wait_recv()

    def multiply(row0, size):
        def tile(i, _):
            column = pl.multiple_of(i * FEATURE_TILE, FEATURE_TILE)
            total = functools.reduce(
                jnp.add,
                [
                    dot(
                        rows_all[b, pl.ds(row0, size), :],
                        weights[b, pl.ds(column, FEATURE_TILE), :],
                        NT,
                    )
                    for b in range(n_dp)
                ],
            )
            out_ref[pl.ds(row0, size), pl.ds(column, FEATURE_TILE)] = total.astype(out_ref.dtype)
            return 0

        lax.fori_loop(0, features // FEATURE_TILE, tile, 0)

    def finish_chunk(i, _):
        row0 = pl.multiple_of(i * CHUNK, 16)
        arrive(row0, CHUNK, i, 3)
        multiply(row0, CHUNK)
        return 0

    lax.fori_loop(0, full, finish_chunk, 0)
    arrive(chunks[-1][0], chunks[-1][1], full, 3)
    multiply(full * CHUNK, rest)

    def sent(copy):
        copy.wait_send()

    for c, (row0, size) in enumerate(chunks):
        for distance in range(n_dp - 1):
            forward(row0, size, c, distance, sent)
    for j, peer in enumerate(seq_peers):
        text_copy(seq, peer, j).wait_send()
        stat_copy(seq, peer, j).wait_send()
        weight_copy(seq, peer, j).wait_send()
        relay_copy(peer, j, img).wait_send()


def body_kernel(
    sizes,
    queries,
    out_grad,
    token_image,
    unnormed_keys,
    values,
    key_gain,
    tile_count,
    key_projection_matrix,
    value_projection_matrix,
):
    n_seq, n_dp, heads, group = sizes
    rows, width = unnormed_keys.shape[1:]
    features = key_projection_matrix.shape[0]
    query_rows = n_seq * group * CAP
    chunk_count = rows // CHUNK + 1
    padded = -(-rows // 16) * 16
    vmem = pl.BlockSpec(memory_space=pltpu.VMEM)
    anywhere = pl.BlockSpec(memory_space=pltpu.HBM)
    dma = pltpu.SemaphoreType.DMA
    result = pl.pallas_call(
        functools.partial(kernel, sizes),
        out_shape=pltpu.VMEM((rows, features), jnp.bfloat16),
        in_specs=[
            vmem,
            pl.BlockSpec(memory_space=pltpu.SMEM),
            vmem,
            vmem,
            vmem,
            vmem,
            vmem,
            anywhere,
            anywhere,
        ],
        out_specs=vmem,
        scratch_shapes=[
            pltpu.VMEM((n_seq, 2, heads, group * CAP, HEAD_WIDTH), jnp.bfloat16),
            pltpu.VMEM((heads, rows, query_rows), jnp.float32),
            pltpu.VMEM((heads, rows, query_rows), jnp.float32),
            pltpu.VMEM((n_seq, 8, heads * query_rows), jnp.float32),
            pltpu.VMEM((n_dp, padded, 2 * width), jnp.bfloat16),
            pltpu.VMEM((n_seq, features, 2 * width), jnp.bfloat16),
            dma((n_seq - 1,)),
            dma((n_seq,)),
            dma((n_seq - 1,)),
            dma((n_seq,)),
            dma((2,)),
            dma((n_seq - 1,)),
            dma((n_seq,)),
            dma((n_seq - 1,)),
            dma((n_seq,)),
            dma((2, n_dp - 1, chunk_count)),
            dma((n_dp, chunk_count)),
        ],
        compiler_params=pltpu.CompilerParams(
            collective_id=0, has_side_effects=True, vmem_limit_bytes=40 * 1024 * 1024
        ),
    )(
        token_image[None],
        tile_count,
        queries,
        out_grad,
        unnormed_keys[0],
        values[0],
        key_gain[None],
        key_projection_matrix,
        value_projection_matrix,
    )
    return result[None]


def body(*args):
    n_seq, n_img, n_dp = (lax.axis_size(name) for name in ("seq", "img", "dp"))
    rows, width = args[3].shape[1:]
    heads = width // HEAD_WIDTH
    group = args[0].shape[1] // width
    fits = n_img == 2 and n_seq == n_dp == 4 and args[7].shape[1] == width and rows % 8 == 0
    if fits and rows % CHUNK and rows % CHUNK % 16 == 8:
        return body_kernel((n_seq, n_dp, heads, group), *args)
    return body_any(*args)


def solution(mesh):
    in_specs = (
        P("seq", "dp"),
        P("seq", "dp"),
        P("seq"),
        P("img", "seq", "dp"),
        P("img", "seq", "dp"),
        P(),
        P(),
        P("dp", "seq"),
        P("dp", "seq"),
    )
    out_specs = P("img", "seq", "dp")
    return jax.shard_map(body, mesh=mesh, in_specs=in_specs, out_specs=out_specs, check_vma=False)
```

```python
import functools

import jax
import jax.numpy as jnp
from jax import lax
from jax.experimental import pallas as pl
from jax.experimental.pallas import tpu as pltpu
from jax.sharding import PartitionSpec as P

QUERY_HEAD_COUNT = 64
KEY_VALUE_HEADS = 8
HEAD_WIDTH = 128
TILE_TOK = 1601
TILE_ROWS = 1608
CAP = 16


epsilon = 1e-05
masked = -1e30


def body_any(
    queries,
    out_grad,
    token_image,
    unnormed_keys,
    values,
    key_gain,
    tile_count,
    key_projection_matrix,
    value_projection_matrix,
):
    image_number = lax.axis_index("img")
    seq_index = lax.axis_index("seq")
    attends = token_image == image_number
    slot_rank = jnp.cumsum(attends.astype(jnp.int32)) - 1
    picker = (
        attends[None, :] & (slot_rank[None, :] == jnp.arange(CAP, dtype=jnp.int32)[:, None])
    ).astype(jnp.bfloat16)
    packed_query = jnp.dot(picker, queries, preferred_element_type=jnp.float32).astype(jnp.bfloat16)
    packed_grad = jnp.dot(picker, out_grad, preferred_element_type=jnp.float32).astype(jnp.bfloat16)
    text_query, text_grad = (
        lax.all_gather(packed_query, "seq", axis=0, tiled=True),
        lax.all_gather(packed_grad, "seq", axis=0, tiled=True),
    )
    key_rows = unnormed_keys.shape[1]
    key_width = unnormed_keys.shape[2]
    key_heads = key_width // HEAD_WIDTH
    group_length = QUERY_HEAD_COUNT // KEY_VALUE_HEADS
    text_rows = text_query.shape[0]
    score_scale = HEAD_WIDTH ** (-0.5)
    unnormed_float = unnormed_keys[0].astype(jnp.float32).reshape(key_rows, key_heads, HEAD_WIDTH)
    inverse = lax.rsqrt(jnp.mean(unnormed_float * unnormed_float, axis=-1, keepdims=True) + epsilon)
    unit_key = unnormed_float * inverse
    normed = (unit_key * key_gain).astype(jnp.bfloat16)
    value_heads = values[0].reshape(key_rows, key_heads, HEAD_WIDTH)
    query_heads = text_query.reshape(text_rows, key_heads, group_length, HEAD_WIDTH)
    grad_heads = text_grad.reshape(text_rows, key_heads, group_length, HEAD_WIDTH)
    row_global = seq_index * key_rows + jnp.arange(key_rows, dtype=jnp.int32)
    tile_limit = jnp.sum(
        jnp.where(jnp.arange(tile_count.shape[0], dtype=jnp.int32) == image_number, tile_count, 0)
    )
    live_rows = (row_global // TILE_ROWS < tile_limit) & (row_global % TILE_ROWS < TILE_TOK)
    scores = (
        jnp.einsum("rhge,khe->hgrk", query_heads, normed, preferred_element_type=jnp.float32)
        * score_scale
    )
    scores = jnp.where(live_rows, scores, masked)
    grad_probs = jnp.einsum(
        "rhge,khe->hgrk", grad_heads, value_heads, preferred_element_type=jnp.float32
    )
    row_top = lax.pmax(jnp.max(scores, axis=-1), "seq")
    exponent = jnp.exp(scores - row_top[..., None])
    row_total = lax.psum(jnp.sum(exponent, axis=-1), "seq")
    probabilities = exponent / row_total[..., None]
    inner_sum = lax.psum(jnp.sum(probabilities * grad_probs, axis=-1), "seq")
    probs_low = probabilities.astype(jnp.bfloat16)
    score_grad = (probabilities * (grad_probs - inner_sum[..., None])).astype(jnp.bfloat16)
    value_gradient = jnp.einsum(
        "hgrk,rhge->khe", probs_low, grad_heads, preferred_element_type=jnp.float32
    )
    normalized_gradient = (
        jnp.einsum("hgrk,rhge->khe", score_grad, query_heads, preferred_element_type=jnp.float32)
        * score_scale
    )
    unit_grad = normalized_gradient * key_gain
    key_gradient = inverse * (
        unit_grad - unit_key * jnp.mean(unit_grad * unit_key, axis=-1, keepdims=True)
    )
    key_reduced_precision = key_gradient.astype(jnp.bfloat16).reshape(key_rows, key_width)
    value_reduced_precision = value_gradient.astype(jnp.bfloat16).reshape(key_rows, key_width)
    key_all, value_all = (
        lax.all_gather(key_reduced_precision, "dp", axis=1, tiled=True),
        lax.all_gather(value_reduced_precision, "dp", axis=1, tiled=True),
    )
    contracting = (((1,), (1,)), ((), ()))
    partial_value = lax.dot_general(
        key_all,
        lax.all_gather(key_projection_matrix, "seq", axis=1, tiled=True),
        contracting,
        preferred_element_type=jnp.float32,
    )
    feature_sum = partial_value + lax.dot_general(
        value_all,
        lax.all_gather(value_projection_matrix, "seq", axis=1, tiled=True),
        contracting,
        preferred_element_type=jnp.float32,
    )
    return feature_sum.astype(jnp.bfloat16)[None]


MESH = pl.DeviceIdType.MESH
NT = (((1,), (1,)), ((), ()))
NN = (((1,), (0,)), ((), ()))
CHUNK = 272
FEATURE_TILE = 256
VMEM_BYTES = 67043328


def dot(a, b, dims):
    return lax.dot_general(a, b, dims, preferred_element_type=jnp.float32)


def kernel(
    sizes,
    image_ref,
    limit_ref,
    query_hbm,
    grad_hbm,
    key_hbm,
    value_hbm,
    gain_ref,
    key_weight_ref,
    value_weight_ref,
    out_ref,
    query_ref,
    grad_ref,
    key_ref,
    value_ref,
    normed_ref,
    text,
    score,
    grad_prob,
    stats,
    rows_all,
    weights,
    load_sem,
    text_send,
    text_recv,
    stat_send,
    stat_recv,
    weight_local,
    weight_send,
    weight_recv,
    relay_send,
    relay_recv,
    row_send,
    row_recv,
):
    n_seq, n_dp, heads, group = sizes
    seq = lax.axis_index("seq")
    img = lax.axis_index("img")
    dp = lax.axis_index("dp")
    rows, width = key_ref.shape
    features = key_weight_ref.shape[0]
    half = features // 2
    stack = group * CAP
    query_rows = n_seq * stack
    full = rows // CHUNK
    rest = rows - full * CHUNK
    padded = rows_all.shape[1]
    chunks = [(c * CHUNK, CHUNK) for c in range(full)] + [(full * CHUNK, padded - full * CHUNK)]
    scale = HEAD_WIDTH ** (-0.5)
    near, far = seq % 2, seq // 2
    seq_peers = [far * 2 + 1 - near, (1 - far) * 2 + near, (1 - far) * 2 + 1 - near]

    loads = [
        pltpu.make_async_copy(source, target, load_sem.at[k])
        for k, (source, target) in enumerate(
            (
                (query_hbm, query_ref),
                (grad_hbm, grad_ref),
                (key_hbm, key_ref),
                (value_hbm, value_ref),
            )
        )
    ]
    for copy in loads:
        copy.start()

    own_weights = [
        pltpu.make_async_copy(
            ref, weights.at[seq, :, pl.ds(k * width, width)], weight_local.at[k]
        )
        for k, ref in enumerate((key_weight_ref, value_weight_ref))
    ]
    barrier = pltpu.get_barrier_semaphore()
    for peer in seq_peers:
        pl.semaphore_signal(barrier, inc=1, device_id={"seq": peer}, device_id_type=MESH)
    pl.semaphore_signal(barrier, inc=1, device_id={"img": 1 - img}, device_id_type=MESH)
    for j in range(1, n_dp):
        pl.semaphore_signal(
            barrier, inc=1, device_id={"dp": lax.rem(dp + j, n_dp)}, device_id_type=MESH
        )

    tokens = image_ref.shape[1]
    attends = image_ref[...] == img
    upper = (
        lax.broadcasted_iota(jnp.int32, (tokens, tokens), 0)
        <= lax.broadcasted_iota(jnp.int32, (tokens, tokens), 1)
    ).astype(jnp.bfloat16)
    counts = dot(
        jnp.broadcast_to(attends.astype(jnp.float32), (CAP, tokens)).astype(jnp.bfloat16), upper, NN
    )
    slot = lax.broadcasted_iota(jnp.int32, (CAP, tokens), 0).astype(jnp.float32) + 1.0
    picker = jnp.where(attends & (counts == slot), 1.0, 0.0).astype(jnp.bfloat16)
    for k, ref in enumerate((query_ref, grad_ref)):
        loads[k].wait()
        packed = dot(picker, ref[...], NN).astype(jnp.bfloat16)
        for h in range(heads):
            for g in range(group):
                column = (h * group + g) * HEAD_WIDTH
                text[seq, k, h, g * CAP : (g + 1) * CAP, :] = packed[:, column : column + HEAD_WIDTH]

    pl.semaphore_wait(barrier, n_seq - 1 + 1 + n_dp - 1)

    def text_copy(owner, peer, j):
        return pltpu.make_async_remote_copy(
            src_ref=text.at[owner],
            dst_ref=text.at[owner],
            send_sem=text_send.at[j],
            recv_sem=text_recv.at[owner],
            device_id={"seq": peer},
            device_id_type=MESH,
        )

    for j, peer in enumerate(seq_peers):
        text_copy(seq, peer, j).start()

    gain = gain_ref[...]
    live_limit = limit_ref[img]

    def unit_of(row0, size, h):
        k = key_ref[pl.ds(row0, size), h * HEAD_WIDTH : (h + 1) * HEAD_WIDTH].astype(jnp.float32)
        inverse = lax.rsqrt(jnp.mean(k * k, axis=-1, keepdims=True) + epsilon)
        return k * inverse, inverse

    def heads_of(k, h):
        return text[:, k, h].reshape(query_rows, HEAD_WIDTH)

    for copy in own_weights:
        copy.start()
    for copy in loads[2:]:
        copy.wait()

    def normalize(row0, size):
        for h in range(heads):
            unit, _ = unit_of(row0, size, h)
            normed_ref[pl.ds(row0, size), h * HEAD_WIDTH : (h + 1) * HEAD_WIDTH] = (
                unit * gain
            ).astype(jnp.bfloat16)

    def over_chunks(act, carry):
        carry = lax.fori_loop(
            0, full, lambda i, c: act(pl.multiple_of(i * CHUNK, 16), CHUNK, c), carry
        )
        return act(full * CHUNK, rest, carry)

    def normalize_chunk(row0, size, carry):
        normalize(row0, size)
        return carry

    over_chunks(normalize_chunk, 0)

    for j, owner in enumerate([seq] + seq_peers):
        if j:
            text_copy(owner, owner, j - 1).wait_recv()
        lanes = pl.ds(pl.multiple_of(owner * stack, stack), stack)

        def first_pass(row0, size, tops):
            new_tops = []
            row = seq * rows + row0 + lax.broadcasted_iota(jnp.int32, (size, 1), 0)
            live = (row // TILE_ROWS < live_limit) & (row % TILE_ROWS < TILE_TOK)
            for h in range(heads):
                normed = normed_ref[pl.ds(row0, size), h * HEAD_WIDTH : (h + 1) * HEAD_WIDTH]
                s = jnp.where(live, dot(normed, text[owner, 0, h], NT) * scale, masked)
                score[h, pl.ds(row0, size), lanes] = s
                new_tops.append(jnp.maximum(tops[h], jnp.max(s, axis=0, keepdims=True)))
            return tuple(new_tops)

        tops = over_chunks(
            first_pass, tuple(jnp.full((1, stack), masked, jnp.float32) for _ in range(heads))
        )

        def second_pass(row0, size, sums):
            new_sums = []
            for h in range(heads):
                e = jnp.exp(score[h, pl.ds(row0, size), lanes] - tops[h])
                v = value_ref[pl.ds(row0, size), h * HEAD_WIDTH : (h + 1) * HEAD_WIDTH]
                p = dot(v, text[owner, 1, h], NT)
                score[h, pl.ds(row0, size), lanes] = e
                grad_prob[h, pl.ds(row0, size), lanes] = p
                new_sums.append(sums[2 * h] + jnp.sum(e, axis=0, keepdims=True))
                new_sums.append(sums[2 * h + 1] + jnp.sum(e * p, axis=0, keepdims=True))
            return tuple(new_sums)

        sums = over_chunks(
            second_pass, tuple(jnp.zeros((1, stack), jnp.float32) for _ in range(2 * heads))
        )
        for h in range(heads):
            columns = pl.ds(pl.multiple_of(h * query_rows + owner * stack, stack), stack)
            stats[seq, 0:1, columns] = tops[h]
            stats[seq, 1:2, columns] = sums[2 * h]
            stats[seq, 2:3, columns] = sums[2 * h + 1]
    stats[seq, 3:8, :] = jnp.zeros((5, heads * query_rows), jnp.float32)

    def stat_copy(owner, peer, j):
        return pltpu.make_async_remote_copy(
            src_ref=stats.at[owner],
            dst_ref=stats.at[owner],
            send_sem=stat_send.at[j],
            recv_sem=stat_recv.at[owner],
            device_id={"seq": peer},
            device_id_type=MESH,
        )

    for j, peer in enumerate(seq_peers):
        stat_copy(seq, peer, j).start()
    for copy in own_weights:
        copy.wait()
    for j, peer in enumerate(seq_peers):
        stat_copy(peer, peer, j).wait_recv()

    def weight_copy(owner, peer, j):
        part = weights.at[owner, pl.ds(pl.multiple_of(img * half, half), half)]
        return pltpu.make_async_remote_copy(
            src_ref=part,
            dst_ref=part,
            send_sem=weight_send.at[j],
            recv_sem=weight_recv.at[owner],
            device_id={"seq": peer},
            device_id_type=MESH,
        )

    def relay_copy(owner, j, which):
        part = weights.at[owner, pl.ds(pl.multiple_of(which * half, half), half)]
        return pltpu.make_async_remote_copy(
            src_ref=part,
            dst_ref=part,
            send_sem=relay_send.at[j],
            recv_sem=relay_recv.at[owner],
            device_id={"img": 1 - img},
            device_id_type=MESH,
        )

    for j, peer in enumerate(seq_peers):
        weight_copy(seq, peer, j).start()

    all_tops = [stats[i, 0:1, :] for i in range(n_seq)]
    top = functools.reduce(jnp.maximum, all_tops)
    factors = [jnp.exp(t - top) for t in all_tops]
    total = sum(f * stats[i, 1:2, :] for i, f in enumerate(factors))
    inner_all = sum(f * stats[i, 2:3, :] for i, f in enumerate(factors)) / total
    own_factor_all = jnp.exp(stats[seq, 0:1, :] - top) / total

    def row_copy(owner, row0, size, c, side, distance):
        part = rows_all.at[owner, pl.ds(row0, size)]
        return pltpu.make_async_remote_copy(
            src_ref=part,
            dst_ref=part,
            send_sem=row_send.at[side, distance, c],
            recv_sem=row_recv.at[owner, c],
            device_id={"dp": dp + 1 if side == 0 else dp - 1},
            device_id_type=MESH,
        )

    def forward(row0, size, c, distance, act):
        for side in range(2):
            owner = dp - distance if side == 0 else dp + distance
            if side == 0:
                sends = (owner >= 0) & (dp < n_dp - 1)
            else:
                sends = (owner < n_dp) & (dp > 0)

            @pl.when(sends)
            def _():
                act(row_copy(owner, row0, size, c, side, distance))

    def arrive(row0, size, c, distance):
        for side in range(2):
            owner = dp - distance if side == 0 else dp + distance

            @pl.when((owner >= 0) & (owner < n_dp))
            def _():
                row_copy(owner, row0, size, c, side, 0).wait_recv()

    def third_pass(row0, size):
        for h in range(heads):
            columns = slice(h * query_rows, (h + 1) * query_rows)
            p = score[h, pl.ds(row0, size), :] * own_factor_all[:, columns]
            g = (p * (grad_prob[h, pl.ds(row0, size), :] - inner_all[:, columns])).astype(jnp.bfloat16)
            value_gradient = dot(p.astype(jnp.bfloat16), heads_of(1, h), NN)
            unit_grad = dot(g, heads_of(0, h), NN) * scale * gain
            unit, inverse = unit_of(row0, size, h)
            key_gradient = inverse * (
                unit_grad - unit * jnp.mean(unit_grad * unit, axis=-1, keepdims=True)
            )
            lane = h * HEAD_WIDTH
            rows_all[dp, pl.ds(row0, size), lane : lane + HEAD_WIDTH] = key_gradient.astype(
                jnp.bfloat16
            )
            lane = lane + width
            rows_all[dp, pl.ds(row0, size), lane : lane + HEAD_WIDTH] = value_gradient.astype(
                jnp.bfloat16
            )

    def start(copy):
        copy.start()

    def own_chunk(i, _):
        row0 = pl.multiple_of(i * CHUNK, 16)
        third_pass(row0, CHUNK)
        forward(row0, CHUNK, i, 0, start)
        return 0

    lax.fori_loop(0, full, own_chunk, 0)
    third_pass(full * CHUNK, rest)
    forward(chunks[-1][0], chunks[-1][1], full, 0, start)

    for c, (row0, size) in enumerate(chunks):
        arrive(row0, size, c, 1)
        forward(row0, size, c, 1, start)
    for j, peer in enumerate(seq_peers):
        weight_copy(peer, peer, j).wait_recv()
        relay_copy(peer, j, img).start()
    for c, (row0, size) in enumerate(chunks):
        arrive(row0, size, c, 2)
        forward(row0, size, c, 2, start)
    for j, peer in enumerate(seq_peers):
        relay_copy(peer, j, 1 - img).wait_recv()

    def multiply(row0, size):
        def tile(i, _):
            column = pl.multiple_of(i * FEATURE_TILE, FEATURE_TILE)
            total = functools.reduce(
                jnp.add,
                [
                    dot(
                        rows_all[b, pl.ds(row0, size), :],
                        weights[b, pl.ds(column, FEATURE_TILE), :],
                        NT,
                    )
                    for b in range(n_dp)
                ],
            )
            out_ref[pl.ds(row0, size), pl.ds(column, FEATURE_TILE)] = total.astype(out_ref.dtype)
            return 0

        lax.fori_loop(0, features // FEATURE_TILE, tile, 0)

    def finish_chunk(i, _):
        row0 = pl.multiple_of(i * CHUNK, 16)
        arrive(row0, CHUNK, i, 3)
        multiply(row0, CHUNK)
        return 0

    lax.fori_loop(0, full, finish_chunk, 0)
    arrive(chunks[-1][0], chunks[-1][1], full, 3)
    multiply(full * CHUNK, rest)

    def sent(copy):
        copy.wait_send()

    for c, (row0, size) in enumerate(chunks):
        for distance in range(n_dp - 1):
            forward(row0, size, c, distance, sent)
    for j, peer in enumerate(seq_peers):
        text_copy(seq, peer, j).wait_send()
        stat_copy(seq, peer, j).wait_send()
        weight_copy(seq, peer, j).wait_send()
        relay_copy(peer, j, img).wait_send()


def body_kernel(
    sizes,
    queries,
    out_grad,
    token_image,
    unnormed_keys,
    values,
    key_gain,
    tile_count,
    key_projection_matrix,
    value_projection_matrix,
):
    n_seq, n_dp, heads, group = sizes
    rows, width = unnormed_keys.shape[1:]
    features = key_projection_matrix.shape[0]
    query_rows = n_seq * group * CAP
    chunk_count = rows // CHUNK + 1
    padded = -(-rows // 16) * 16
    vmem = pl.BlockSpec(memory_space=pltpu.VMEM)
    anywhere = pl.BlockSpec(memory_space=pltpu.HBM)
    dma = pltpu.SemaphoreType.DMA
    result = pl.pallas_call(
        functools.partial(kernel, sizes),
        out_shape=pltpu.VMEM((rows, features), jnp.bfloat16),
        in_specs=[
            vmem,
            pl.BlockSpec(memory_space=pltpu.SMEM),
            anywhere,
            anywhere,
            anywhere,
            anywhere,
            vmem,
            anywhere,
            anywhere,
        ],
        out_specs=vmem,
        scratch_shapes=[
            pltpu.VMEM(queries.shape, jnp.bfloat16),
            pltpu.VMEM(queries.shape, jnp.bfloat16),
            pltpu.VMEM((rows, width), jnp.bfloat16),
            pltpu.VMEM((rows, width), jnp.bfloat16),
            pltpu.VMEM((rows, width), jnp.bfloat16),
            pltpu.VMEM((n_seq, 2, heads, group * CAP, HEAD_WIDTH), jnp.bfloat16),
            pltpu.VMEM((heads, rows, query_rows), jnp.float32),
            pltpu.VMEM((heads, rows, query_rows), jnp.float32),
            pltpu.VMEM((n_seq, 8, heads * query_rows), jnp.float32),
            pltpu.VMEM((n_dp, padded, 2 * width), jnp.bfloat16),
            pltpu.VMEM((n_seq, features, 2 * width), jnp.bfloat16),
            dma((4,)),
            dma((n_seq - 1,)),
            dma((n_seq,)),
            dma((n_seq - 1,)),
            dma((n_seq,)),
            dma((2,)),
            dma((n_seq - 1,)),
            dma((n_seq,)),
            dma((n_seq - 1,)),
            dma((n_seq,)),
            dma((2, n_dp - 1, chunk_count)),
            dma((n_dp, chunk_count)),
        ],
        compiler_params=pltpu.CompilerParams(
            collective_id=0, has_side_effects=True, vmem_limit_bytes=VMEM_BYTES - 2 * rows * features
        ),
    )(
        token_image[None],
        tile_count,
        queries,
        out_grad,
        unnormed_keys[0],
        values[0],
        key_gain[None],
        key_projection_matrix,
        value_projection_matrix,
    )
    return result[None]


def body(*args):
    n_seq, n_img, n_dp = (lax.axis_size(name) for name in ("seq", "img", "dp"))
    rows, width = args[3].shape[1:]
    heads = width // HEAD_WIDTH
    group = args[0].shape[1] // width
    fits = n_img == 2 and n_seq == n_dp == 4 and args[7].shape[1] == width and rows % 8 == 0
    if fits and rows % CHUNK and rows % CHUNK % 16 == 8:
        return body_kernel((n_seq, n_dp, heads, group), *args)
    return body_any(*args)


def solution(mesh):
    in_specs = (
        P("seq", "dp"),
        P("seq", "dp"),
        P("seq"),
        P("img", "seq", "dp"),
        P("img", "seq", "dp"),
        P(),
        P(),
        P("dp", "seq"),
        P("dp", "seq"),
    )
    out_specs = P("img", "seq", "dp")
    return jax.shard_map(body, mesh=mesh, in_specs=in_specs, out_specs=out_specs, check_vma=False)
```

```python
import functools

import jax
import jax.numpy as jnp
from jax import lax
from jax.experimental import pallas as pl
from jax.experimental.pallas import tpu as pltpu
from jax.sharding import PartitionSpec as P

QUERY_HEAD_COUNT = 64
KEY_VALUE_HEADS = 8
HEAD_WIDTH = 128
TILE_TOK = 1601
TILE_ROWS = 1608
CAP = 16


epsilon = 1e-05
masked = -1e30


def body_any(
    queries,
    out_grad,
    token_image,
    unnormed_keys,
    values,
    key_gain,
    tile_count,
    key_projection_matrix,
    value_projection_matrix,
):
    image_number = lax.axis_index("img")
    seq_index = lax.axis_index("seq")
    attends = token_image == image_number
    slot_rank = jnp.cumsum(attends.astype(jnp.int32)) - 1
    picker = (
        attends[None, :] & (slot_rank[None, :] == jnp.arange(CAP, dtype=jnp.int32)[:, None])
    ).astype(jnp.bfloat16)
    packed_query = jnp.dot(picker, queries, preferred_element_type=jnp.float32).astype(jnp.bfloat16)
    packed_grad = jnp.dot(picker, out_grad, preferred_element_type=jnp.float32).astype(jnp.bfloat16)
    text_query, text_grad = (
        lax.all_gather(packed_query, "seq", axis=0, tiled=True),
        lax.all_gather(packed_grad, "seq", axis=0, tiled=True),
    )
    key_rows = unnormed_keys.shape[1]
    key_width = unnormed_keys.shape[2]
    key_heads = key_width // HEAD_WIDTH
    group_length = QUERY_HEAD_COUNT // KEY_VALUE_HEADS
    text_rows = text_query.shape[0]
    score_scale = HEAD_WIDTH ** (-0.5)
    unnormed_float = unnormed_keys[0].astype(jnp.float32).reshape(key_rows, key_heads, HEAD_WIDTH)
    inverse = lax.rsqrt(jnp.mean(unnormed_float * unnormed_float, axis=-1, keepdims=True) + epsilon)
    unit_key = unnormed_float * inverse
    normed = (unit_key * key_gain).astype(jnp.bfloat16)
    value_heads = values[0].reshape(key_rows, key_heads, HEAD_WIDTH)
    query_heads = text_query.reshape(text_rows, key_heads, group_length, HEAD_WIDTH)
    grad_heads = text_grad.reshape(text_rows, key_heads, group_length, HEAD_WIDTH)
    row_global = seq_index * key_rows + jnp.arange(key_rows, dtype=jnp.int32)
    tile_limit = jnp.sum(
        jnp.where(jnp.arange(tile_count.shape[0], dtype=jnp.int32) == image_number, tile_count, 0)
    )
    live_rows = (row_global // TILE_ROWS < tile_limit) & (row_global % TILE_ROWS < TILE_TOK)
    scores = (
        jnp.einsum("rhge,khe->hgrk", query_heads, normed, preferred_element_type=jnp.float32)
        * score_scale
    )
    scores = jnp.where(live_rows, scores, masked)
    grad_probs = jnp.einsum(
        "rhge,khe->hgrk", grad_heads, value_heads, preferred_element_type=jnp.float32
    )
    row_top = lax.pmax(jnp.max(scores, axis=-1), "seq")
    exponent = jnp.exp(scores - row_top[..., None])
    row_total = lax.psum(jnp.sum(exponent, axis=-1), "seq")
    probabilities = exponent / row_total[..., None]
    inner_sum = lax.psum(jnp.sum(probabilities * grad_probs, axis=-1), "seq")
    probs_low = probabilities.astype(jnp.bfloat16)
    score_grad = (probabilities * (grad_probs - inner_sum[..., None])).astype(jnp.bfloat16)
    value_gradient = jnp.einsum(
        "hgrk,rhge->khe", probs_low, grad_heads, preferred_element_type=jnp.float32
    )
    normalized_gradient = (
        jnp.einsum("hgrk,rhge->khe", score_grad, query_heads, preferred_element_type=jnp.float32)
        * score_scale
    )
    unit_grad = normalized_gradient * key_gain
    key_gradient = inverse * (
        unit_grad - unit_key * jnp.mean(unit_grad * unit_key, axis=-1, keepdims=True)
    )
    key_reduced_precision = key_gradient.astype(jnp.bfloat16).reshape(key_rows, key_width)
    value_reduced_precision = value_gradient.astype(jnp.bfloat16).reshape(key_rows, key_width)
    key_all, value_all = (
        lax.all_gather(key_reduced_precision, "dp", axis=1, tiled=True),
        lax.all_gather(value_reduced_precision, "dp", axis=1, tiled=True),
    )
    contracting = (((1,), (1,)), ((), ()))
    partial_value = lax.dot_general(
        key_all,
        lax.all_gather(key_projection_matrix, "seq", axis=1, tiled=True),
        contracting,
        preferred_element_type=jnp.float32,
    )
    feature_sum = partial_value + lax.dot_general(
        value_all,
        lax.all_gather(value_projection_matrix, "seq", axis=1, tiled=True),
        contracting,
        preferred_element_type=jnp.float32,
    )
    return feature_sum.astype(jnp.bfloat16)[None]


MESH = pl.DeviceIdType.MESH
NT = (((1,), (1,)), ((), ()))
NN = (((1,), (0,)), ((), ()))
CHUNK = 240
FEATURE_TILE = 256
VMEM_BYTES = 67043328


def dot(a, b, dims):
    return lax.dot_general(a, b, dims, preferred_element_type=jnp.float32)


def multiply(rows_all, weights, row0, size, out_ref, out_row0):
    def tile(i, _):
        column = pl.multiple_of(i * FEATURE_TILE, FEATURE_TILE)
        total = functools.reduce(
            jnp.add,
            [
                dot(
                    rows_all[b, pl.ds(row0, size), :],
                    weights[b, pl.ds(column, FEATURE_TILE), :],
                    NT,
                )
                for b in range(rows_all.shape[0])
            ],
        )
        out_ref[pl.ds(out_row0, size), pl.ds(column, FEATURE_TILE)] = total.astype(out_ref.dtype)
        return 0

    lax.fori_loop(0, weights.shape[1] // FEATURE_TILE, tile, 0)


def finish_kernel(done_ref, rows_all, weights, out_ref, last_ref, sems):
    done = done_ref.shape[0]
    rest = last_ref.shape[0]
    first = pltpu.make_async_copy(done_ref, out_ref.at[pl.ds(0, done)], sems.at[0])
    first.start()
    multiply(rows_all, weights, done, rest, last_ref, 0)
    second = pltpu.make_async_copy(last_ref, out_ref.at[pl.ds(done, rest)], sems.at[1])
    second.start()
    first.wait()
    second.wait()


def kernel(
    sizes,
    image_ref,
    limit_ref,
    query_hbm,
    grad_hbm,
    key_hbm,
    value_hbm,
    gain_ref,
    key_weight_ref,
    value_weight_ref,
    out_ref,
    rows_all,
    weights,
    query_ref,
    grad_ref,
    key_ref,
    value_ref,
    normed_ref,
    text,
    score,
    grad_prob,
    stats,
    load_sem,
    text_send,
    text_recv,
    stat_send,
    stat_recv,
    weight_local,
    weight_send,
    weight_recv,
    relay_send,
    relay_recv,
    row_send,
    row_recv,
):
    n_seq, n_dp, heads, group = sizes
    seq = lax.axis_index("seq")
    img = lax.axis_index("img")
    dp = lax.axis_index("dp")
    rows, width = key_ref.shape
    features = key_weight_ref.shape[0]
    half = features // 2
    stack = group * CAP
    query_rows = n_seq * stack
    full = rows // CHUNK
    rest = rows - full * CHUNK
    padded = rows_all.shape[1]
    chunks = [(c * CHUNK, CHUNK) for c in range(full)] + [(full * CHUNK, padded - full * CHUNK)]
    scale = HEAD_WIDTH ** (-0.5)
    near, far = seq % 2, seq // 2
    seq_peers = [far * 2 + 1 - near, (1 - far) * 2 + near, (1 - far) * 2 + 1 - near]

    loads = [
        pltpu.make_async_copy(source, target, load_sem.at[k])
        for k, (source, target) in enumerate(
            (
                (query_hbm, query_ref),
                (grad_hbm, grad_ref),
                (key_hbm, key_ref),
                (value_hbm, value_ref),
            )
        )
    ]
    for copy in loads:
        copy.start()

    own_weights = [
        pltpu.make_async_copy(
            ref, weights.at[seq, :, pl.ds(k * width, width)], weight_local.at[k]
        )
        for k, ref in enumerate((key_weight_ref, value_weight_ref))
    ]
    barrier = pltpu.get_barrier_semaphore()
    for peer in seq_peers:
        pl.semaphore_signal(barrier, inc=1, device_id={"seq": peer}, device_id_type=MESH)
    pl.semaphore_signal(barrier, inc=1, device_id={"img": 1 - img}, device_id_type=MESH)
    for j in range(1, n_dp):
        pl.semaphore_signal(
            barrier, inc=1, device_id={"dp": lax.rem(dp + j, n_dp)}, device_id_type=MESH
        )

    tokens = image_ref.shape[1]
    attends = image_ref[...] == img
    upper = (
        lax.broadcasted_iota(jnp.int32, (tokens, tokens), 0)
        <= lax.broadcasted_iota(jnp.int32, (tokens, tokens), 1)
    ).astype(jnp.bfloat16)
    counts = dot(
        jnp.broadcast_to(attends.astype(jnp.float32), (CAP, tokens)).astype(jnp.bfloat16), upper, NN
    )
    slot = lax.broadcasted_iota(jnp.int32, (CAP, tokens), 0).astype(jnp.float32) + 1.0
    picker = jnp.where(attends & (counts == slot), 1.0, 0.0).astype(jnp.bfloat16)
    for k, ref in enumerate((query_ref, grad_ref)):
        loads[k].wait()
        packed = dot(picker, ref[...], NN).astype(jnp.bfloat16)
        for h in range(heads):
            for g in range(group):
                column = (h * group + g) * HEAD_WIDTH
                text[seq, k, h, g * CAP : (g + 1) * CAP, :] = packed[:, column : column + HEAD_WIDTH]

    pl.semaphore_wait(barrier, n_seq - 1 + 1 + n_dp - 1)

    def text_copy(owner, peer, j):
        return pltpu.make_async_remote_copy(
            src_ref=text.at[owner],
            dst_ref=text.at[owner],
            send_sem=text_send.at[j],
            recv_sem=text_recv.at[owner],
            device_id={"seq": peer},
            device_id_type=MESH,
        )

    for j, peer in enumerate(seq_peers):
        text_copy(seq, peer, j).start()

    gain = gain_ref[...]
    live_limit = limit_ref[img]

    def unit_of(row0, size, h):
        k = key_ref[pl.ds(row0, size), h * HEAD_WIDTH : (h + 1) * HEAD_WIDTH].astype(jnp.float32)
        inverse = lax.rsqrt(jnp.mean(k * k, axis=-1, keepdims=True) + epsilon)
        return k * inverse, inverse

    def heads_of(k, h):
        return text[:, k, h].reshape(query_rows, HEAD_WIDTH)

    for copy in own_weights:
        copy.start()
    for copy in loads[2:]:
        copy.wait()

    def normalize(row0, size):
        for h in range(heads):
            unit, _ = unit_of(row0, size, h)
            normed_ref[pl.ds(row0, size), h * HEAD_WIDTH : (h + 1) * HEAD_WIDTH] = (
                unit * gain
            ).astype(jnp.bfloat16)

    def over_chunks(act, carry):
        carry = lax.fori_loop(
            0, full, lambda i, c: act(pl.multiple_of(i * CHUNK, 16), CHUNK, c), carry
        )
        return act(full * CHUNK, rest, carry)

    def normalize_chunk(row0, size, carry):
        normalize(row0, size)
        return carry

    over_chunks(normalize_chunk, 0)

    for j, owner in enumerate([seq] + seq_peers):
        if j:
            text_copy(owner, owner, j - 1).wait_recv()
        lanes = pl.ds(pl.multiple_of(owner * stack, stack), stack)

        def first_pass(row0, size, tops):
            new_tops = []
            row = seq * rows + row0 + lax.broadcasted_iota(jnp.int32, (size, 1), 0)
            live = (row // TILE_ROWS < live_limit) & (row % TILE_ROWS < TILE_TOK)
            for h in range(heads):
                normed = normed_ref[pl.ds(row0, size), h * HEAD_WIDTH : (h + 1) * HEAD_WIDTH]
                s = jnp.where(live, dot(normed, text[owner, 0, h], NT) * scale, masked)
                score[h, pl.ds(row0, size), lanes] = s
                new_tops.append(jnp.maximum(tops[h], jnp.max(s, axis=0, keepdims=True)))
            return tuple(new_tops)

        tops = over_chunks(
            first_pass, tuple(jnp.full((1, stack), masked, jnp.float32) for _ in range(heads))
        )

        def second_pass(row0, size, sums):
            new_sums = []
            for h in range(heads):
                e = jnp.exp(score[h, pl.ds(row0, size), lanes] - tops[h])
                v = value_ref[pl.ds(row0, size), h * HEAD_WIDTH : (h + 1) * HEAD_WIDTH]
                p = dot(v, text[owner, 1, h], NT)
                score[h, pl.ds(row0, size), lanes] = e
                grad_prob[h, pl.ds(row0, size), lanes] = p
                new_sums.append(sums[2 * h] + jnp.sum(e, axis=0, keepdims=True))
                new_sums.append(sums[2 * h + 1] + jnp.sum(e * p, axis=0, keepdims=True))
            return tuple(new_sums)

        sums = over_chunks(
            second_pass, tuple(jnp.zeros((1, stack), jnp.float32) for _ in range(2 * heads))
        )
        for h in range(heads):
            columns = pl.ds(pl.multiple_of(h * query_rows + owner * stack, stack), stack)
            stats[seq, 0:1, columns] = tops[h]
            stats[seq, 1:2, columns] = sums[2 * h]
            stats[seq, 2:3, columns] = sums[2 * h + 1]
    stats[seq, 3:8, :] = jnp.zeros((5, heads * query_rows), jnp.float32)

    def stat_copy(owner, peer, j):
        return pltpu.make_async_remote_copy(
            src_ref=stats.at[owner],
            dst_ref=stats.at[owner],
            send_sem=stat_send.at[j],
            recv_sem=stat_recv.at[owner],
            device_id={"seq": peer},
            device_id_type=MESH,
        )

    for j, peer in enumerate(seq_peers):
        stat_copy(seq, peer, j).start()
    for copy in own_weights:
        copy.wait()
    for j, peer in enumerate(seq_peers):
        stat_copy(peer, peer, j).wait_recv()

    def weight_copy(owner, peer, j):
        part = weights.at[owner, pl.ds(pl.multiple_of(img * half, half), half)]
        return pltpu.make_async_remote_copy(
            src_ref=part,
            dst_ref=part,
            send_sem=weight_send.at[j],
            recv_sem=weight_recv.at[owner],
            device_id={"seq": peer},
            device_id_type=MESH,
        )

    def relay_copy(owner, j, which):
        part = weights.at[owner, pl.ds(pl.multiple_of(which * half, half), half)]
        return pltpu.make_async_remote_copy(
            src_ref=part,
            dst_ref=part,
            send_sem=relay_send.at[j],
            recv_sem=relay_recv.at[owner],
            device_id={"img": 1 - img},
            device_id_type=MESH,
        )

    for j, peer in enumerate(seq_peers):
        weight_copy(seq, peer, j).start()

    all_tops = [stats[i, 0:1, :] for i in range(n_seq)]
    top = functools.reduce(jnp.maximum, all_tops)
    factors = [jnp.exp(t - top) for t in all_tops]
    total = sum(f * stats[i, 1:2, :] for i, f in enumerate(factors))
    inner_all = sum(f * stats[i, 2:3, :] for i, f in enumerate(factors)) / total
    own_factor_all = jnp.exp(stats[seq, 0:1, :] - top) / total

    def row_copy(owner, row0, size, c, side, distance):
        part = rows_all.at[owner, pl.ds(row0, size)]
        return pltpu.make_async_remote_copy(
            src_ref=part,
            dst_ref=part,
            send_sem=row_send.at[side, distance, c],
            recv_sem=row_recv.at[owner, c],
            device_id={"dp": dp + 1 if side == 0 else dp - 1},
            device_id_type=MESH,
        )

    def forward(row0, size, c, distance, act):
        for side in range(2):
            owner = dp - distance if side == 0 else dp + distance
            if side == 0:
                sends = (owner >= 0) & (dp < n_dp - 1)
            else:
                sends = (owner < n_dp) & (dp > 0)

            @pl.when(sends)
            def _():
                act(row_copy(owner, row0, size, c, side, distance))

    def arrive(row0, size, c, distance):
        for side in range(2):
            owner = dp - distance if side == 0 else dp + distance

            @pl.when((owner >= 0) & (owner < n_dp))
            def _():
                row_copy(owner, row0, size, c, side, 0).wait_recv()

    def third_pass(row0, size):
        for h in range(heads):
            columns = slice(h * query_rows, (h + 1) * query_rows)
            p = score[h, pl.ds(row0, size), :] * own_factor_all[:, columns]
            g = (p * (grad_prob[h, pl.ds(row0, size), :] - inner_all[:, columns])).astype(jnp.bfloat16)
            value_gradient = dot(p.astype(jnp.bfloat16), heads_of(1, h), NN)
            unit_grad = dot(g, heads_of(0, h), NN) * scale * gain
            unit, inverse = unit_of(row0, size, h)
            key_gradient = inverse * (
                unit_grad - unit * jnp.mean(unit_grad * unit, axis=-1, keepdims=True)
            )
            lane = h * HEAD_WIDTH
            rows_all[dp, pl.ds(row0, size), lane : lane + HEAD_WIDTH] = key_gradient.astype(
                jnp.bfloat16
            )
            lane = lane + width
            rows_all[dp, pl.ds(row0, size), lane : lane + HEAD_WIDTH] = value_gradient.astype(
                jnp.bfloat16
            )

    def start(copy):
        copy.start()

    def own_chunk(i, _):
        row0 = pl.multiple_of(i * CHUNK, 16)
        third_pass(row0, CHUNK)
        forward(row0, CHUNK, i, 0, start)
        return 0

    lax.fori_loop(0, full, own_chunk, 0)
    third_pass(full * CHUNK, rest)
    forward(chunks[-1][0], chunks[-1][1], full, 0, start)

    for c, (row0, size) in enumerate(chunks):
        arrive(row0, size, c, 1)
        forward(row0, size, c, 1, start)
    for j, peer in enumerate(seq_peers):
        weight_copy(peer, peer, j).wait_recv()
        relay_copy(peer, j, img).start()
    for c, (row0, size) in enumerate(chunks):
        arrive(row0, size, c, 2)
        forward(row0, size, c, 2, start)
    for j, peer in enumerate(seq_peers):
        relay_copy(peer, j, 1 - img).wait_recv()

    def finish_chunk(i, _):
        row0 = pl.multiple_of(i * CHUNK, 16)
        arrive(row0, CHUNK, i, 3)
        multiply(rows_all, weights, row0, CHUNK, out_ref, row0)
        return 0

    lax.fori_loop(0, full, finish_chunk, 0)
    arrive(chunks[-1][0], chunks[-1][1], full, 3)

    def sent(copy):
        copy.wait_send()

    for c, (row0, size) in enumerate(chunks):
        for distance in range(n_dp - 1):
            forward(row0, size, c, distance, sent)
    for j, peer in enumerate(seq_peers):
        text_copy(seq, peer, j).wait_send()
        stat_copy(seq, peer, j).wait_send()
        weight_copy(seq, peer, j).wait_send()
        relay_copy(peer, j, img).wait_send()


def body_kernel(
    sizes,
    queries,
    out_grad,
    token_image,
    unnormed_keys,
    values,
    key_gain,
    tile_count,
    key_projection_matrix,
    value_projection_matrix,
):
    n_seq, n_dp, heads, group = sizes
    rows, width = unnormed_keys.shape[1:]
    features = key_projection_matrix.shape[0]
    query_rows = n_seq * group * CAP
    chunk_count = rows // CHUNK + 1
    padded = -(-rows // 16) * 16
    vmem = pl.BlockSpec(memory_space=pltpu.VMEM)
    anywhere = pl.BlockSpec(memory_space=pltpu.HBM)
    dma = pltpu.SemaphoreType.DMA
    done = rows // CHUNK * CHUNK
    kept = 2 * (done * features + n_dp * padded * 2 * width + n_seq * features * 2 * width)
    finished, rows_all, weights = pl.pallas_call(
        functools.partial(kernel, sizes),
        out_shape=(
            pltpu.VMEM((done, features), jnp.bfloat16),
            pltpu.VMEM((n_dp, padded, 2 * width), jnp.bfloat16),
            pltpu.VMEM((n_seq, features, 2 * width), jnp.bfloat16),
        ),
        in_specs=[
            vmem,
            pl.BlockSpec(memory_space=pltpu.SMEM),
            anywhere,
            anywhere,
            anywhere,
            anywhere,
            vmem,
            anywhere,
            anywhere,
        ],
        out_specs=(vmem, vmem, vmem),
        scratch_shapes=[
            pltpu.VMEM(queries.shape, jnp.bfloat16),
            pltpu.VMEM(queries.shape, jnp.bfloat16),
            pltpu.VMEM((rows, width), jnp.bfloat16),
            pltpu.VMEM((rows, width), jnp.bfloat16),
            pltpu.VMEM((rows, width), jnp.bfloat16),
            pltpu.VMEM((n_seq, 2, heads, group * CAP, HEAD_WIDTH), jnp.bfloat16),
            pltpu.VMEM((heads, rows, query_rows), jnp.float32),
            pltpu.VMEM((heads, rows, query_rows), jnp.float32),
            pltpu.VMEM((n_seq, 8, heads * query_rows), jnp.float32),
            dma((4,)),
            dma((n_seq - 1,)),
            dma((n_seq,)),
            dma((n_seq - 1,)),
            dma((n_seq,)),
            dma((2,)),
            dma((n_seq - 1,)),
            dma((n_seq,)),
            dma((n_seq - 1,)),
            dma((n_seq,)),
            dma((2, n_dp - 1, chunk_count)),
            dma((n_dp, chunk_count)),
        ],
        compiler_params=pltpu.CompilerParams(
            collective_id=0, has_side_effects=True, vmem_limit_bytes=VMEM_BYTES - kept
        ),
    )(
        token_image[None],
        tile_count,
        queries,
        out_grad,
        unnormed_keys[0],
        values[0],
        key_gain[None],
        key_projection_matrix,
        value_projection_matrix,
    )
    result = pl.pallas_call(
        finish_kernel,
        out_shape=jax.ShapeDtypeStruct((rows, features), jnp.bfloat16),
        in_specs=[vmem, vmem, vmem],
        out_specs=pl.BlockSpec(memory_space=pltpu.HBM),
        scratch_shapes=[pltpu.VMEM((rows - done, features), jnp.bfloat16), dma((2,))],
        compiler_params=pltpu.CompilerParams(vmem_limit_bytes=8 * 1024 * 1024),
    )(finished, rows_all, weights)
    return result[None]


def body(*args):
    n_seq, n_img, n_dp = (lax.axis_size(name) for name in ("seq", "img", "dp"))
    rows, width = args[3].shape[1:]
    heads = width // HEAD_WIDTH
    group = args[0].shape[1] // width
    fits = n_img == 2 and n_seq == n_dp == 4 and args[7].shape[1] == width and rows % 8 == 0
    if fits and rows % CHUNK and rows % CHUNK % 16 == 8:
        return body_kernel((n_seq, n_dp, heads, group), *args)
    return body_any(*args)


def solution(mesh):
    in_specs = (
        P("seq", "dp"),
        P("seq", "dp"),
        P("seq"),
        P("img", "seq", "dp"),
        P("img", "seq", "dp"),
        P(),
        P(),
        P("dp", "seq"),
        P("dp", "seq"),
    )
    out_specs = P("img", "seq", "dp")
    return jax.shard_map(body, mesh=mesh, in_specs=in_specs, out_specs=out_specs, check_vma=False)
```

```python
import functools

import jax
import jax.numpy as jnp
from jax import lax
from jax.experimental import pallas as pl
from jax.experimental.pallas import tpu as pltpu
from jax.sharding import PartitionSpec as P

QUERY_HEAD_COUNT = 64
KEY_VALUE_HEADS = 8
HEAD_WIDTH = 128
TILE_TOK = 1601
TILE_ROWS = 1608
CAP = 16


epsilon = 1e-05
masked = -1e30


def body_any(
    queries,
    out_grad,
    token_image,
    unnormed_keys,
    values,
    key_gain,
    tile_count,
    key_projection_matrix,
    value_projection_matrix,
):
    image_number = lax.axis_index("img")
    seq_index = lax.axis_index("seq")
    attends = token_image == image_number
    slot_rank = jnp.cumsum(attends.astype(jnp.int32)) - 1
    picker = (
        attends[None, :] & (slot_rank[None, :] == jnp.arange(CAP, dtype=jnp.int32)[:, None])
    ).astype(jnp.bfloat16)
    packed_query = jnp.dot(picker, queries, preferred_element_type=jnp.float32).astype(jnp.bfloat16)
    packed_grad = jnp.dot(picker, out_grad, preferred_element_type=jnp.float32).astype(jnp.bfloat16)
    text_query, text_grad = (
        lax.all_gather(packed_query, "seq", axis=0, tiled=True),
        lax.all_gather(packed_grad, "seq", axis=0, tiled=True),
    )
    key_rows = unnormed_keys.shape[1]
    key_width = unnormed_keys.shape[2]
    key_heads = key_width // HEAD_WIDTH
    group_length = QUERY_HEAD_COUNT // KEY_VALUE_HEADS
    text_rows = text_query.shape[0]
    score_scale = HEAD_WIDTH ** (-0.5)
    unnormed_float = unnormed_keys[0].astype(jnp.float32).reshape(key_rows, key_heads, HEAD_WIDTH)
    inverse = lax.rsqrt(jnp.mean(unnormed_float * unnormed_float, axis=-1, keepdims=True) + epsilon)
    unit_key = unnormed_float * inverse
    normed = (unit_key * key_gain).astype(jnp.bfloat16)
    value_heads = values[0].reshape(key_rows, key_heads, HEAD_WIDTH)
    query_heads = text_query.reshape(text_rows, key_heads, group_length, HEAD_WIDTH)
    grad_heads = text_grad.reshape(text_rows, key_heads, group_length, HEAD_WIDTH)
    row_global = seq_index * key_rows + jnp.arange(key_rows, dtype=jnp.int32)
    tile_limit = jnp.sum(
        jnp.where(jnp.arange(tile_count.shape[0], dtype=jnp.int32) == image_number, tile_count, 0)
    )
    live_rows = (row_global // TILE_ROWS < tile_limit) & (row_global % TILE_ROWS < TILE_TOK)
    scores = (
        jnp.einsum("rhge,khe->hgrk", query_heads, normed, preferred_element_type=jnp.float32)
        * score_scale
    )
    scores = jnp.where(live_rows, scores, masked)
    grad_probs = jnp.einsum(
        "rhge,khe->hgrk", grad_heads, value_heads, preferred_element_type=jnp.float32
    )
    row_top = lax.pmax(jnp.max(scores, axis=-1), "seq")
    exponent = jnp.exp(scores - row_top[..., None])
    row_total = lax.psum(jnp.sum(exponent, axis=-1), "seq")
    probabilities = exponent / row_total[..., None]
    inner_sum = lax.psum(jnp.sum(probabilities * grad_probs, axis=-1), "seq")
    probs_low = probabilities.astype(jnp.bfloat16)
    score_grad = (probabilities * (grad_probs - inner_sum[..., None])).astype(jnp.bfloat16)
    value_gradient = jnp.einsum(
        "hgrk,rhge->khe", probs_low, grad_heads, preferred_element_type=jnp.float32
    )
    normalized_gradient = (
        jnp.einsum("hgrk,rhge->khe", score_grad, query_heads, preferred_element_type=jnp.float32)
        * score_scale
    )
    unit_grad = normalized_gradient * key_gain
    key_gradient = inverse * (
        unit_grad - unit_key * jnp.mean(unit_grad * unit_key, axis=-1, keepdims=True)
    )
    key_reduced_precision = key_gradient.astype(jnp.bfloat16).reshape(key_rows, key_width)
    value_reduced_precision = value_gradient.astype(jnp.bfloat16).reshape(key_rows, key_width)
    key_all, value_all = (
        lax.all_gather(key_reduced_precision, "dp", axis=1, tiled=True),
        lax.all_gather(value_reduced_precision, "dp", axis=1, tiled=True),
    )
    contracting = (((1,), (1,)), ((), ()))
    partial_value = lax.dot_general(
        key_all,
        lax.all_gather(key_projection_matrix, "seq", axis=1, tiled=True),
        contracting,
        preferred_element_type=jnp.float32,
    )
    feature_sum = partial_value + lax.dot_general(
        value_all,
        lax.all_gather(value_projection_matrix, "seq", axis=1, tiled=True),
        contracting,
        preferred_element_type=jnp.float32,
    )
    return feature_sum.astype(jnp.bfloat16)[None]


MESH = pl.DeviceIdType.MESH
NT = (((1,), (1,)), ((), ()))
NN = (((1,), (0,)), ((), ()))
CHUNK = 272
FEATURE_TILE = 256
VMEM_BYTES = 67043328


def dot(a, b, dims):
    return lax.dot_general(a, b, dims, preferred_element_type=jnp.float32)


def kernel(
    sizes,
    image_ref,
    limit_ref,
    query_hbm,
    grad_hbm,
    key_hbm,
    value_hbm,
    gain_ref,
    key_weight_ref,
    value_weight_ref,
    out_ref,
    query_ref,
    grad_ref,
    key_ref,
    value_ref,
    normed_ref,
    partial,
    text,
    score,
    grad_prob,
    stats,
    rows_all,
    weights,
    load_sem,
    text_send,
    text_recv,
    stat_send,
    stat_recv,
    weight_local,
    weight_send,
    weight_recv,
    relay_send,
    relay_recv,
    row_send,
    row_recv,
):
    n_seq, n_dp, heads, group = sizes
    seq = lax.axis_index("seq")
    img = lax.axis_index("img")
    dp = lax.axis_index("dp")
    rows, width = key_ref.shape
    features = key_weight_ref.shape[0]
    half = features // 2
    stack = group * CAP
    query_rows = n_seq * stack
    full = rows // CHUNK
    rest = rows - full * CHUNK
    padded = rows_all.shape[1]
    chunks = [(c * CHUNK, CHUNK) for c in range(full)] + [(full * CHUNK, padded - full * CHUNK)]
    scale = HEAD_WIDTH ** (-0.5)
    near, far = seq % 2, seq // 2
    seq_peers = [far * 2 + 1 - near, (1 - far) * 2 + near, (1 - far) * 2 + 1 - near]

    loads = [
        pltpu.make_async_copy(source, target, load_sem.at[k])
        for k, (source, target) in enumerate(
            (
                (query_hbm, query_ref),
                (grad_hbm, grad_ref),
                (key_hbm, key_ref),
                (value_hbm, value_ref),
            )
        )
    ]
    for copy in loads:
        copy.start()

    own_weights = [
        pltpu.make_async_copy(
            ref, weights.at[seq, :, pl.ds(k * width, width)], weight_local.at[k]
        )
        for k, ref in enumerate((key_weight_ref, value_weight_ref))
    ]
    barrier = pltpu.get_barrier_semaphore()
    for peer in seq_peers:
        pl.semaphore_signal(barrier, inc=1, device_id={"seq": peer}, device_id_type=MESH)
    pl.semaphore_signal(barrier, inc=1, device_id={"img": 1 - img}, device_id_type=MESH)
    for j in range(1, n_dp):
        pl.semaphore_signal(
            barrier, inc=1, device_id={"dp": lax.rem(dp + j, n_dp)}, device_id_type=MESH
        )

    tokens = image_ref.shape[1]
    attends = image_ref[...] == img
    upper = (
        lax.broadcasted_iota(jnp.int32, (tokens, tokens), 0)
        <= lax.broadcasted_iota(jnp.int32, (tokens, tokens), 1)
    ).astype(jnp.bfloat16)
    counts = dot(
        jnp.broadcast_to(attends.astype(jnp.float32), (CAP, tokens)).astype(jnp.bfloat16), upper, NN
    )
    slot = lax.broadcasted_iota(jnp.int32, (CAP, tokens), 0).astype(jnp.float32) + 1.0
    picker = jnp.where(attends & (counts == slot), 1.0, 0.0).astype(jnp.bfloat16)
    for k, ref in enumerate((query_ref, grad_ref)):
        loads[k].wait()
        packed = dot(picker, ref[...], NN).astype(jnp.bfloat16)
        for h in range(heads):
            for g in range(group):
                column = (h * group + g) * HEAD_WIDTH
                text[seq, k, h, g * CAP : (g + 1) * CAP, :] = packed[:, column : column + HEAD_WIDTH]

    pl.semaphore_wait(barrier, n_seq - 1 + 1 + n_dp - 1)

    def text_copy(owner, peer, j):
        return pltpu.make_async_remote_copy(
            src_ref=text.at[owner],
            dst_ref=text.at[owner],
            send_sem=text_send.at[j],
            recv_sem=text_recv.at[owner],
            device_id={"seq": peer},
            device_id_type=MESH,
        )

    for j, peer in enumerate(seq_peers):
        text_copy(seq, peer, j).start()

    gain = gain_ref[...]
    live_limit = limit_ref[img]

    def unit_of(row0, size, h):
        k = key_ref[pl.ds(row0, size), h * HEAD_WIDTH : (h + 1) * HEAD_WIDTH].astype(jnp.float32)
        inverse = lax.rsqrt(jnp.mean(k * k, axis=-1, keepdims=True) + epsilon)
        return k * inverse, inverse

    def heads_of(k, h):
        return text[:, k, h].reshape(query_rows, HEAD_WIDTH)

    for copy in own_weights:
        copy.start()
    for copy in loads[2:]:
        copy.wait()

    def normalize(row0, size):
        for h in range(heads):
            unit, _ = unit_of(row0, size, h)
            normed_ref[pl.ds(row0, size), h * HEAD_WIDTH : (h + 1) * HEAD_WIDTH] = (
                unit * gain
            ).astype(jnp.bfloat16)

    def over_chunks(act, carry):
        carry = lax.fori_loop(
            0, full, lambda i, c: act(pl.multiple_of(i * CHUNK, 16), CHUNK, c), carry
        )
        return act(full * CHUNK, rest, carry)

    def normalize_chunk(row0, size, carry):
        normalize(row0, size)
        return carry

    over_chunks(normalize_chunk, 0)

    for j, owner in enumerate([seq] + seq_peers):
        if j:
            text_copy(owner, owner, j - 1).wait_recv()
        lanes = pl.ds(pl.multiple_of(owner * stack, stack), stack)

        def first_pass(row0, size, tops):
            new_tops = []
            row = seq * rows + row0 + lax.broadcasted_iota(jnp.int32, (size, 1), 0)
            live = (row // TILE_ROWS < live_limit) & (row % TILE_ROWS < TILE_TOK)
            for h in range(heads):
                normed = normed_ref[pl.ds(row0, size), h * HEAD_WIDTH : (h + 1) * HEAD_WIDTH]
                s = jnp.where(live, dot(normed, text[owner, 0, h], NT) * scale, masked)
                score[h, pl.ds(row0, size), lanes] = s
                new_tops.append(jnp.maximum(tops[h], jnp.max(s, axis=0, keepdims=True)))
            return tuple(new_tops)

        tops = over_chunks(
            first_pass, tuple(jnp.full((1, stack), masked, jnp.float32) for _ in range(heads))
        )

        def second_pass(row0, size, sums):
            new_sums = []
            for h in range(heads):
                e = jnp.exp(score[h, pl.ds(row0, size), lanes] - tops[h])
                v = value_ref[pl.ds(row0, size), h * HEAD_WIDTH : (h + 1) * HEAD_WIDTH]
                p = dot(v, text[owner, 1, h], NT)
                score[h, pl.ds(row0, size), lanes] = e
                grad_prob[h, pl.ds(row0, size), lanes] = p
                new_sums.append(sums[2 * h] + jnp.sum(e, axis=0, keepdims=True))
                new_sums.append(sums[2 * h + 1] + jnp.sum(e * p, axis=0, keepdims=True))
            return tuple(new_sums)

        sums = over_chunks(
            second_pass, tuple(jnp.zeros((1, stack), jnp.float32) for _ in range(2 * heads))
        )
        for h in range(heads):
            columns = pl.ds(pl.multiple_of(h * query_rows + owner * stack, stack), stack)
            stats[seq, 0:1, columns] = tops[h]
            stats[seq, 1:2, columns] = sums[2 * h]
            stats[seq, 2:3, columns] = sums[2 * h + 1]
    stats[seq, 3:8, :] = jnp.zeros((5, heads * query_rows), jnp.float32)

    def stat_copy(owner, peer, j):
        return pltpu.make_async_remote_copy(
            src_ref=stats.at[owner],
            dst_ref=stats.at[owner],
            send_sem=stat_send.at[j],
            recv_sem=stat_recv.at[owner],
            device_id={"seq": peer},
            device_id_type=MESH,
        )

    for j, peer in enumerate(seq_peers):
        stat_copy(seq, peer, j).start()
    for copy in own_weights:
        copy.wait()
    for j, peer in enumerate(seq_peers):
        stat_copy(peer, peer, j).wait_recv()

    def weight_copy(owner, peer, j):
        part = weights.at[owner, pl.ds(pl.multiple_of(img * half, half), half)]
        return pltpu.make_async_remote_copy(
            src_ref=part,
            dst_ref=part,
            send_sem=weight_send.at[j],
            recv_sem=weight_recv.at[owner],
            device_id={"seq": peer},
            device_id_type=MESH,
        )

    def relay_copy(owner, j, which):
        part = weights.at[owner, pl.ds(pl.multiple_of(which * half, half), half)]
        return pltpu.make_async_remote_copy(
            src_ref=part,
            dst_ref=part,
            send_sem=relay_send.at[j],
            recv_sem=relay_recv.at[owner],
            device_id={"img": 1 - img},
            device_id_type=MESH,
        )

    for j, peer in enumerate(seq_peers):
        weight_copy(seq, peer, j).start()

    all_tops = [stats[i, 0:1, :] for i in range(n_seq)]
    top = functools.reduce(jnp.maximum, all_tops)
    factors = [jnp.exp(t - top) for t in all_tops]
    total = sum(f * stats[i, 1:2, :] for i, f in enumerate(factors))
    inner_all = sum(f * stats[i, 2:3, :] for i, f in enumerate(factors)) / total
    own_factor_all = jnp.exp(stats[seq, 0:1, :] - top) / total

    def row_copy(owner, row0, size, c, side, distance):
        part = rows_all.at[owner, pl.ds(row0, size)]
        return pltpu.make_async_remote_copy(
            src_ref=part,
            dst_ref=part,
            send_sem=row_send.at[side, distance, c],
            recv_sem=row_recv.at[owner, c],
            device_id={"dp": dp + 1 if side == 0 else dp - 1},
            device_id_type=MESH,
        )

    def forward(row0, size, c, distance, act):
        for side in range(2):
            owner = dp - distance if side == 0 else dp + distance
            if side == 0:
                sends = (owner >= 0) & (dp < n_dp - 1)
            else:
                sends = (owner < n_dp) & (dp > 0)

            @pl.when(sends)
            def _():
                act(row_copy(owner, row0, size, c, side, distance))

    def arrive(row0, size, c, distance):
        for side in range(2):
            owner = dp - distance if side == 0 else dp + distance

            @pl.when((owner >= 0) & (owner < n_dp))
            def _():
                row_copy(owner, row0, size, c, side, 0).wait_recv()

    def third_pass(row0, size):
        for h in range(heads):
            columns = slice(h * query_rows, (h + 1) * query_rows)
            p = score[h, pl.ds(row0, size), :] * own_factor_all[:, columns]
            g = (p * (grad_prob[h, pl.ds(row0, size), :] - inner_all[:, columns])).astype(jnp.bfloat16)
            value_gradient = dot(p.astype(jnp.bfloat16), heads_of(1, h), NN)
            unit_grad = dot(g, heads_of(0, h), NN) * scale * gain
            unit, inverse = unit_of(row0, size, h)
            key_gradient = inverse * (
                unit_grad - unit * jnp.mean(unit_grad * unit, axis=-1, keepdims=True)
            )
            lane = h * HEAD_WIDTH
            rows_all[dp, pl.ds(row0, size), lane : lane + HEAD_WIDTH] = key_gradient.astype(
                jnp.bfloat16
            )
            lane = lane + width
            rows_all[dp, pl.ds(row0, size), lane : lane + HEAD_WIDTH] = value_gradient.astype(
                jnp.bfloat16
            )

    def start(copy):
        copy.start()

    def own_chunk(i, _):
        row0 = pl.multiple_of(i * CHUNK, 16)
        third_pass(row0, CHUNK)
        forward(row0, CHUNK, i, 0, start)
        return 0

    lax.fori_loop(0, full, own_chunk, 0)
    third_pass(full * CHUNK, rest)
    forward(chunks[-1][0], chunks[-1][1], full, 0, start)

    for c, (row0, size) in enumerate(chunks):
        arrive(row0, size, c, 1)
        forward(row0, size, c, 1, start)
    for j, peer in enumerate(seq_peers):
        weight_copy(peer, peer, j).wait_recv()
        relay_copy(peer, j, img).start()
    for c, (row0, size) in enumerate(chunks):
        arrive(row0, size, c, 2)
        forward(row0, size, c, 2, start)
    for j, peer in enumerate(seq_peers):
        relay_copy(peer, j, 1 - img).wait_recv()

    def multiply(row0, size):
        def tile(i, _):
            column = pl.multiple_of(i * FEATURE_TILE, FEATURE_TILE)
            total = functools.reduce(
                jnp.add,
                [
                    dot(
                        rows_all[b, pl.ds(row0, size), :],
                        weights[b, pl.ds(column, FEATURE_TILE), :],
                        NT,
                    )
                    for b in range(n_dp)
                ],
            )
            out_ref[pl.ds(row0, size), pl.ds(column, FEATURE_TILE)] = total.astype(out_ref.dtype)
            return 0

        lax.fori_loop(0, features // FEATURE_TILE, tile, 0)

    def finish_chunk(i, _):
        row0 = pl.multiple_of(i * CHUNK, 16)
        arrive(row0, CHUNK, i, 3)
        multiply(row0, CHUNK)
        return 0

    upper_half = dp // (n_dp // 2)
    farthest = (n_dp - 1) * (1 - upper_half)

    def last_product(block, column):
        return dot(
            rows_all[block, full * CHUNK : rows, :],
            weights[block, pl.ds(column, FEATURE_TILE), :],
            NT,
        )

    def partial_tile(i, _):
        column = pl.multiple_of(i * FEATURE_TILE, FEATURE_TILE)
        partial[:, pl.ds(column, FEATURE_TILE)] = functools.reduce(
            jnp.add, [last_product(upper_half + b, column) for b in range(n_dp - 1)]
        )
        return 0

    def last_tile(i, _):
        column = pl.multiple_of(i * FEATURE_TILE, FEATURE_TILE)
        total = partial[:, pl.ds(column, FEATURE_TILE)] + last_product(farthest, column)
        out_ref[full * CHUNK : rows, pl.ds(column, FEATURE_TILE)] = total.astype(out_ref.dtype)
        return 0

    lax.fori_loop(0, features // FEATURE_TILE, partial_tile, 0)
    lax.fori_loop(0, full, finish_chunk, 0)
    arrive(chunks[-1][0], chunks[-1][1], full, 3)
    lax.fori_loop(0, features // FEATURE_TILE, last_tile, 0)

    def sent(copy):
        copy.wait_send()

    for c, (row0, size) in enumerate(chunks):
        for distance in range(n_dp - 1):
            forward(row0, size, c, distance, sent)
    for j, peer in enumerate(seq_peers):
        text_copy(seq, peer, j).wait_send()
        stat_copy(seq, peer, j).wait_send()
        weight_copy(seq, peer, j).wait_send()
        relay_copy(peer, j, img).wait_send()


def body_kernel(
    sizes,
    queries,
    out_grad,
    token_image,
    unnormed_keys,
    values,
    key_gain,
    tile_count,
    key_projection_matrix,
    value_projection_matrix,
):
    n_seq, n_dp, heads, group = sizes
    rows, width = unnormed_keys.shape[1:]
    features = key_projection_matrix.shape[0]
    query_rows = n_seq * group * CAP
    chunk_count = rows // CHUNK + 1
    padded = -(-rows // 16) * 16
    vmem = pl.BlockSpec(memory_space=pltpu.VMEM)
    anywhere = pl.BlockSpec(memory_space=pltpu.HBM)
    dma = pltpu.SemaphoreType.DMA
    result = pl.pallas_call(
        functools.partial(kernel, sizes),
        out_shape=pltpu.VMEM((rows, features), jnp.bfloat16),
        in_specs=[
            vmem,
            pl.BlockSpec(memory_space=pltpu.SMEM),
            anywhere,
            anywhere,
            anywhere,
            anywhere,
            vmem,
            anywhere,
            anywhere,
        ],
        out_specs=vmem,
        scratch_shapes=[
            pltpu.VMEM(queries.shape, jnp.bfloat16),
            pltpu.VMEM(queries.shape, jnp.bfloat16),
            pltpu.VMEM((rows, width), jnp.bfloat16),
            pltpu.VMEM((rows, width), jnp.bfloat16),
            pltpu.VMEM((rows, width), jnp.bfloat16),
            pltpu.VMEM((rows % CHUNK, features), jnp.float32),
            pltpu.VMEM((n_seq, 2, heads, group * CAP, HEAD_WIDTH), jnp.bfloat16),
            pltpu.VMEM((heads, rows, query_rows), jnp.float32),
            pltpu.VMEM((heads, rows, query_rows), jnp.float32),
            pltpu.VMEM((n_seq, 8, heads * query_rows), jnp.float32),
            pltpu.VMEM((n_dp, padded, 2 * width), jnp.bfloat16),
            pltpu.VMEM((n_seq, features, 2 * width), jnp.bfloat16),
            dma((4,)),
            dma((n_seq - 1,)),
            dma((n_seq,)),
            dma((n_seq - 1,)),
            dma((n_seq,)),
            dma((2,)),
            dma((n_seq - 1,)),
            dma((n_seq,)),
            dma((n_seq - 1,)),
            dma((n_seq,)),
            dma((2, n_dp - 1, chunk_count)),
            dma((n_dp, chunk_count)),
        ],
        compiler_params=pltpu.CompilerParams(
            collective_id=0, has_side_effects=True, vmem_limit_bytes=VMEM_BYTES - 2 * rows * features
        ),
    )(
        token_image[None],
        tile_count,
        queries,
        out_grad,
        unnormed_keys[0],
        values[0],
        key_gain[None],
        key_projection_matrix,
        value_projection_matrix,
    )
    return result[None]


def body(*args):
    n_seq, n_img, n_dp = (lax.axis_size(name) for name in ("seq", "img", "dp"))
    rows, width = args[3].shape[1:]
    heads = width // HEAD_WIDTH
    group = args[0].shape[1] // width
    fits = n_img == 2 and n_seq == n_dp == 4 and args[7].shape[1] == width and rows % 8 == 0
    if fits and rows % CHUNK and rows % CHUNK % 16 == 8:
        return body_kernel((n_seq, n_dp, heads, group), *args)
    return body_any(*args)


def solution(mesh):
    in_specs = (
        P("seq", "dp"),
        P("seq", "dp"),
        P("seq"),
        P("img", "seq", "dp"),
        P("img", "seq", "dp"),
        P(),
        P(),
        P("dp", "seq"),
        P("dp", "seq"),
    )
    out_specs = P("img", "seq", "dp")
    return jax.shard_map(body, mesh=mesh, in_specs=in_specs, out_specs=out_specs, check_vma=False)
```
